256 devices in a mesh: dp: 16 (over z_hi, y, core), expert: 16 (over x, z_lo).
Axes of the slice: x: 4, y: 4, z: 8 (z_hi: 2, z_lo: 4; z = z_hi * 4 + z_lo), core: 2. Of those that a mesh axis runs over, the one named last changes fastest.
Arguments:
- images: bfloat16 [1024, 256, 1280], P(('dp', 'expert')), may hold values from -16 to 16
- router: bfloat16 [1280, 128], replicated, as said below
- w_in: bfloat16 [256, 1280, 1280], P(('dp', 'expert')), may hold values from -0.15625 to 0.15625
- w_out: bfloat16 [256, 1280, 1280], P(('dp', 'expert')), may hold values from -0.125 to 0.125
- keep_bits: int32 [1024, 256, 128], P(None, ('dp', 'expert')), may hold values from 0 to 1023, as said below
Outputs:
- mixed: bfloat16 [1024, 256, 1280], P(('dp', 'expert'))
The draws below stay inside these ranges and needn't reach their ends.
Inputs may be any that keep to these rules, and one draw needn't show every extreme that they name: `router`: each entry within 18 / sqrt(1280) in magnitude. `keep_bits`: bit i of word w stands for hidden unit 10 * w + i.
All inputs are finite; a program needn't handle non-finite values.
Results may differ from the reference program's by a relative error of at most 0.017.
Values may be sent and summed in bfloat16 or wider, within the bound.
A program may use at most 128 MiB of HBM per device.

```python
import math
import jax
import jax.numpy as jnp
from jax import lax

D = 1280
FF = 2560
M = 256
SPLIT = 2
HALF = 1280
E = 128
IMAGES = 1024
N_DP = 16


def router_table(key):
    values = jax.random.normal(jax.random.fold_in(key, 101), (D, E), jnp.float32)
    return jnp.clip(values, -6.0, 6.0) * (3.0 / math.sqrt(D))


def draw_router(key, part):
    return router_table(key).astype(jnp.bfloat16)


def draw_images(key, part):
    base = jax.random.normal(jax.random.fold_in(key, 202), (IMAGES, M, D), jnp.float32)
    return jnp.clip(base, -6.0, 6.0).astype(jnp.bfloat16)


def draw_keep_bits(key, part):
    shape = (IMAGES, SPLIT * E, HALF // 10)
    first = jax.random.randint(jax.random.fold_in(key, 301), shape, 0, 1024)
    second = jax.random.randint(jax.random.fold_in(key, 302), shape, 0, 1024)
    third = jax.random.randint(jax.random.fold_in(key, 303), shape, 0, 1024)
    return jnp.bitwise_or(jnp.bitwise_or(first, second), third).astype(jnp.int32)


def steps_of(rng, dims, cuts, least, top_value):
    def one(position, parts):
        heights = jax.random.uniform(jax.random.fold_in(jax.random.fold_in(rng, 6), position), (parts,), jnp.float32, least / len(cuts), top_value / len(cuts))
        return jnp.repeat(jnp.exp(heights), dims[position] // parts).reshape((-1,) + (1,) * (len(dims) - position - 1))

    gain = one(*cuts[0])
    for cut in cuts[1:]:
        gain = gain * one(*cut)
    return gain


def noise(rng, shape, scale, bound, shards=(), held_as=jnp.bfloat16):
    entries = jax.random.normal(rng, shape, jnp.float32) * scale
    if len(shards) > 0:
        entries = steps_of(rng, shape, shards, -0.22, 0.18) * entries
    return jnp.clip(entries, min=-bound, max=bound).astype(held_as)


def setup_inputs(seed: int = 0) -> dict:
    seeds = jax.random.split(jax.random.key(seed), 6)
    images = draw_images(jax.random.fold_in(seeds[5], 71), 0)
    router = draw_router(jax.random.fold_in(seeds[5], 71), 0)
    w_in = noise(seeds[2], (SPLIT * E, D, HALF), D ** -0.5, 0.15625, ((0, 256),))
    w_out = noise(seeds[3], (SPLIT * E, HALF, D), FF ** -0.5, 0.125, ((0, 256),))
    keep_bits = draw_keep_bits(jax.random.fold_in(seeds[5], 71), 0)
    return dict(images=images, router=router, w_in=w_in, w_out=w_out, keep_bits=keep_bits)


keep_rate = 0.875


def unpack_flags(words):
    shifts = jnp.arange(10, dtype=jnp.int32)
    flags = jnp.right_shift(words[..., None], shifts) & 1
    return flags.reshape(words.shape[:-1] + (words.shape[-1] * 10,)).astype(jnp.float32)


def mix_block(block, router):
    logits = jnp.einsum("bmd,de->bme", block.astype(jnp.float32), router.astype(jnp.float32))
    dispatch = jax.nn.softmax(logits, axis=1).astype(jnp.bfloat16)
    combine = jax.nn.softmax(logits, axis=2).astype(jnp.bfloat16)
    slot_values = jnp.einsum("bme,bmd->bed", dispatch.astype(jnp.float32), block.astype(jnp.float32))
    return slot_values.astype(jnp.bfloat16), combine


def reference(images, router, w_in, w_out, keep_bits):
    grouped = images.reshape(N_DP, IMAGES // N_DP, M, D)
    slot_blocks, combine = lax.map(lambda block: mix_block(block, router), grouped)
    slot_values = slot_blocks.reshape(IMAGES, E, D)

    def expert_rows(index):
        slot_rows = lax.dynamic_index_in_dim(slot_values, index, 1, keepdims=False)
        total = jnp.zeros((IMAGES, D), jnp.float32)
        for half_index in range(SPLIT):
            piece = (SPLIT * index + half_index).astype(jnp.int32)
            first = lax.dynamic_index_in_dim(w_in, piece, 0, keepdims=False)
            second = lax.dynamic_index_in_dim(w_out, piece, 0, keepdims=False)
            kept_units = unpack_flags(lax.dynamic_index_in_dim(keep_bits, piece, 1, keepdims=False))
            pre_act = jnp.dot(slot_rows, first, preferred_element_type=jnp.float32)
            hidden = (jax.nn.gelu(pre_act) * kept_units * (1.0 / keep_rate)).astype(jnp.bfloat16)
            partial_value = jnp.dot(hidden, second, preferred_element_type=jnp.float32).astype(jnp.bfloat16)
            total = total + partial_value.astype(jnp.float32)
        return total.astype(jnp.bfloat16)

    expert_out = lax.map(expert_rows, jnp.arange(E, dtype=jnp.int32))
    expert_out = expert_out.reshape(E, N_DP, IMAGES // N_DP, D)

    def finish(block_index):
        outputs = lax.dynamic_index_in_dim(expert_out, block_index, 1, keepdims=False)
        weights = lax.dynamic_index_in_dim(combine, block_index, 0, keepdims=False)
        mixed = jnp.einsum("bme,ebd->bmd", weights.astype(jnp.float32), outputs.astype(jnp.float32))
        return mixed.astype(jnp.bfloat16)

    mixed = lax.map(finish, jnp.arange(N_DP, dtype=jnp.int32))
    return mixed.reshape(IMAGES, M, D)
```

```python
import jax
import jax.numpy as jnp
from jax import lax
from jax.sharding import PartitionSpec as P

SPLIT = 2


keep_rate = 0.875


def unpack_flags(words):
    shifts = jnp.arange(10, dtype=jnp.int32)
    flags = jnp.right_shift(words[..., None], shifts) & 1
    return flags.reshape(words.shape[:-1] + (words.shape[-1] * 10,)).astype(jnp.float32)


def expert_piece(slot_rows, w_in, w_out, kept_units):
    pre_act = jnp.dot(slot_rows, w_in[0], preferred_element_type=jnp.float32)
    hidden = (jax.nn.gelu(pre_act) * kept_units * (1.0 / keep_rate)).astype(jnp.bfloat16)
    return jnp.dot(hidden, w_out[0], preferred_element_type=jnp.float32).astype(jnp.bfloat16)


def on_device(images, router, w_in, w_out, keep_bits):
    image_count = images.shape[0]
    width = images.shape[2]
    experts = router.shape[1]
    both = ("dp", "expert")
    logits = jnp.einsum("bmd,de->bme", images, router, preferred_element_type=jnp.float32)
    dispatch = jax.nn.softmax(logits, axis=1).astype(jnp.bfloat16)
    combine = jax.nn.softmax(logits, axis=2).astype(jnp.bfloat16)
    slot_values = jnp.einsum(
        "bme,bmd->ebd", dispatch, images, preferred_element_type=jnp.float32
    ).astype(jnp.bfloat16)
    kept_units = unpack_flags(keep_bits[:, 0, :])
    doubled = jnp.repeat(slot_values, SPLIT, axis=0)
    arrived = lax.all_to_all(doubled, both, split_axis=0, concat_axis=0, tiled=True)
    partial_value = expert_piece(arrived.reshape(-1, width), w_in, w_out, kept_units)
    returned = lax.all_to_all(
        partial_value.reshape(-1, image_count, width), both, split_axis=0, concat_axis=0, tiled=True
    )
    paired = returned.reshape(experts, SPLIT, image_count, width)
    expert_out = paired.astype(jnp.float32).sum(axis=1).astype(jnp.bfloat16)
    mixed = jnp.einsum("bme,ebd->bmd", combine, expert_out, preferred_element_type=jnp.float32)
    return mixed.astype(jnp.bfloat16)


def solution(mesh):
    placed = (
        P(("dp", "expert"), None, None),
        P(),
        P(("dp", "expert"), None, None),
        P(("dp", "expert"), None, None),
        P(None, ("dp", "expert"), None),
    )
    return jax.shard_map(
        on_device,
        mesh=mesh,
        in_specs=placed,
        out_specs=P(("dp", "expert"), None, None),
        check_vma=False,
    )
```

```python
import functools

import jax
import jax.numpy as jnp
import numpy as np
from jax import lax
from jax.experimental import pallas as pl
from jax.experimental.pallas import tpu as pltpu
from jax.sharding import PartitionSpec as P

GROUPS = 4
ROWS = 8
PAIRS = 4
IMG = 4
PATCHES = 256
D = 1280
E = 128
IMAGES = 1024
TILE = 256
MESH = pl.DeviceIdType.MESH
KEEP_RATE = 0.875
BF16 = jnp.bfloat16
F32 = jnp.float32


def slot_order():
    table = np.zeros((GROUPS * ROWS * PAIRS * IMG, IMG * E), np.float32)
    for y in range(4):
        for s in range(ROWS):
            for q in range(PAIRS):
                expert = (q // 2) * 64 + y * 16 + (s // 4) * 8 + (s % 4) * 2 + q % 2
                for b in range(IMG):
                    table[((y * ROWS + s) * PAIRS + q) * IMG + b, b * E + expert] = 1.0
    return table


def pair_order():
    table = np.zeros((128, 128), np.float32)
    for q in range(PAIRS):
        for s in range(ROWS):
            for b in range(IMG):
                table[(q * ROWS + s) * IMG + b, (s * PAIRS + q) * IMG + b] = 1.0
    return table


def bit_table():
    table = np.zeros((256, D), np.float32)
    for w in range(128):
        for i in range(10):
            table[w, 10 * w + i] = 32.0 / 2**i
            table[128 + w, 10 * w + i] = 1.0 / 2**i
    return table


def step_along_y(g):
    return g + lax.div(g, 2) * (1 - 2 * lax.rem(g, 2))


def kernel(
    img_h, router_h, w1_h, w2_h, kb_h, order_h, pairs_h, bits_h,
    out_h, spread_h,
    img, router, w1, w2, kb, order, pairs, bits, words, logits, raw, slots,
    xa, za, rows, part, other, total, back, xb, hidden, keep, spread,
    load_sem, xa_send, xa_recv, z_send, z_recv, f_send, f_recv,
    q_send, q_recv, t_send, t_recv, xb_send, xb_recv, out_sem,
):
    dp = lax.axis_index("dp")
    ex = lax.axis_index("expert")
    core = lax.rem(dp, 2)
    y = lax.rem(lax.div(dp, 2), 4)
    z = lax.div(dp, 8) * 4 + lax.rem(ex, 4)
    x = lax.div(ex, 4)
    me = core * 4 + x
    pair = lax.div(z, 2)
    sg = 2 * lax.rem(z, 2) - 1

    def at(s, yy, zz):
        return (
            lax.div(zz, 4) * 8 + yy * 2 + lax.div(s, 4),
            lax.rem(s, 4) * 4 + lax.rem(zz, 4),
        )

    def along_z(step):
        return lax.rem(z + step * sg + 8, 8)

    def along_y(step):
        return lax.rem(y + step + 4, 4)

    loads = [
        (img_h.at[0], img.at[0]),
        (router_h, router),
        (img_h.at[1], img.at[1]),
        (img_h.at[2], img.at[2]),
        (img_h.at[3], img.at[3]),
        (order_h, order),
        (pairs_h, pairs),
        (kb_h, kb),
        (bits_h, bits),
        (w1_h.at[0], w1),
        (w2_h.at[0], w2),
    ]
    copies = [
        pltpu.make_async_copy(src, dst, load_sem.at[i]) for i, (src, dst) in enumerate(loads)
    ]
    for copy in copies:
        copy.start()

    barrier = pltpu.get_barrier_semaphore()
    partners = []
    for dy in range(4):
        for i in range(ROWS):
            if dy or i:
                partners.append(at(lax.rem(me + i, ROWS), along_y(dy), z))
    for step in (1, 2, 3, -1, -2):
        partners.append(at(me, y, along_z(step)))
    for partner in partners:
        pl.semaphore_signal(barrier, inc=1, device_id=partner, device_id_type=MESH)

    for b in range(IMG):
        if b == 0:
            copies[0].wait()
            copies[1].wait()
        else:
            copies[1 + b].wait()
        scores = jnp.dot(img[b], router[...], preferred_element_type=F32)
        logits[b] = scores
        top = jnp.max(scores, axis=0, keepdims=True)
        grown = jnp.exp(scores - top)
        share = (grown / jnp.sum(grown, axis=0, keepdims=True)).astype(BF16)
        for n in range(D // TILE):
            cols = pl.ds(n * TILE, TILE)
            raw[pl.ds(b * E, E), cols] = lax.dot_general(
                share, img[b, :, cols], (((0,), (0,)), ((), ())), preferred_element_type=F32
            ).astype(BF16)

    copies[5].wait()
    for g in range(GROUPS):
        dy = (0, 1, 3, 2)[g]
        yy = along_y(dy)
        pick = order[pl.ds(pl.multiple_of(yy * 128, 128), 128), :]
        for n in range(D // TILE):
            cols = pl.ds(n * TILE, TILE)
            slots[g, :, :, cols] = (
                jnp.dot(pick, raw[:, cols], preferred_element_type=F32)
                .astype(BF16)
                .reshape(ROWS, 16, TILE)
            )
        if g == 0:
            pl.semaphore_wait(barrier, len(partners))
        for i in range(ROWS):
            s = lax.rem(me + i, ROWS)
            if g == 0 and i == 0:
                pltpu.make_async_copy(slots.at[g, s], xa.at[g, me], xa_recv.at[g]).start()
            else:
                pltpu.make_async_remote_copy(
                    slots.at[g, s], xa.at[g, me], xa_send.at[g], xa_recv.at[g],
                    device_id=at(s, yy, z), device_id_type=MESH,
                ).start()

    for b in range(IMG):
        scores = logits[b]
        grown = jnp.exp(scores - jnp.max(scores, axis=1, keepdims=True))
        share = (grown / jnp.sum(grown, axis=1, keepdims=True)).astype(BF16)
        spread[pl.ds(b * PATCHES, PATCHES), :] = lax.dot_general(
            share, order[:, pl.ds(b * E, E)], (((1,), (1,)), ((), ())), preferred_element_type=F32
        ).astype(BF16)
    spread_out = pltpu.make_async_copy(spread, spread_h, out_sem)
    spread_out.start()

    copies[7].wait()
    words[:, pl.ds(0, 128)] = jnp.right_shift(kb[...], 5).astype(F32).astype(BF16)
    words[:, pl.ds(128, 128)] = jnp.bitwise_and(kb[...], 31).astype(F32).astype(BF16)
    for i in (6, 8, 9, 10):
        copies[i].wait()

    def arrived(ref, sem):
        pltpu.make_async_copy(ref, ref, sem).wait()

    def send(src, dst, send_sem, recv_sem, zz):
        pltpu.make_async_remote_copy(
            src, dst, send_sem, recv_sem, device_id=at(me, y, zz), device_id_type=MESH
        ).start()

    def dispatch(g):
        arrived(xa.at[g], xa_recv.at[g])
        for n in range(D // TILE):
            cols = pl.ds(n * TILE, TILE)
            za[g, :, :, cols] = (
                jnp.dot(
                    pairs[...], xa[g, :, :, cols].reshape(128, TILE), preferred_element_type=F32
                )
                .astype(BF16)
                .reshape(PAIRS, 32, TILE)
            )
        send(za.at[g, pair], rows.at[g, 4], z_send.at[g, 0], z_recv.at[g, 0], along_z(-1))
        for slot, step in ((3, 3), (2, -2), (1, 1)):
            zz = along_z(step)
            send(
                za.at[g, lax.div(zz, 2)], rows.at[g, slot],
                z_send.at[g, slot], z_recv.at[g, slot], zz,
            )
        rows[g, 0] = za[g, pair]

    def keep_flags(g):
        r = lax.broadcasted_iota(jnp.int32, (256, 1), 0)
        j = jnp.right_shift(r, 5)
        s = jnp.bitwise_and(jnp.right_shift(r, 2), 7)
        zz = jnp.bitwise_and(jnp.where(j < 4, z + j * sg, z - (j - 3) * sg) + 8, 7)
        yy = along_y(-step_along_y(g))
        group = (jnp.right_shift(zz, 2) * 8 + yy * 2 + jnp.right_shift(s, 2)) * 16
        device = group + jnp.bitwise_and(s, 3) * 4 + jnp.bitwise_and(zz, 3)
        image = device * IMG + jnp.bitwise_and(r, 3)
        c = lax.broadcasted_iota(jnp.int32, (256, IMAGES), 1)
        pick = jnp.where(c == image, 1.0, 0.0).astype(BF16)
        mine = jnp.dot(pick, words[...], preferred_element_type=F32).astype(BF16)

        def tile(n, carry):
            cols = pl.ds(pl.multiple_of(n * TILE, TILE), TILE)
            value = jnp.dot(mine, bits[:, cols], preferred_element_type=F32)
            flag = jnp.bitwise_and(value.astype(jnp.int32), 1)
            keep[:, cols] = flag.astype(F32).astype(BF16)
            return carry

        lax.fori_loop(0, D // TILE, tile, 0)

    def forward(g):
        for j in (3, 2, 1):
            arrived(rows.at[g, j], z_recv.at[g, j])
            send(
                rows.at[g, j], rows.at[g, 4 + j], f_send.at[g, j], f_recv.at[g, j], along_z(-1)
            )

    def experts(g):
        keep_flags(g)
        arrived(rows.at[g, 4], z_recv.at[g, 0])
        for j in (1, 2, 3):
            arrived(rows.at[g, 4 + j], f_recv.at[g, j])

        def first(n, carry):
            cols = pl.ds(pl.multiple_of(n * TILE, TILE), TILE)
            value = jnp.dot(rows[g].reshape(256, D), w1[:, cols], preferred_element_type=F32)
            flag = keep[:, cols].astype(F32)
            hidden[:, cols] = (jax.nn.gelu(value) * flag * (1.0 / KEEP_RATE)).astype(BF16)
            return carry

        def second(n, carry):
            cols = pl.ds(pl.multiple_of(n * TILE, TILE), TILE)
            value = jnp.dot(hidden[...], w2[:, cols], preferred_element_type=F32)
            part[g, :, :, cols] = value.astype(BF16).reshape(8, 32, TILE)
            return carry

        lax.fori_loop(0, D // TILE, first, 0)
        lax.fori_loop(0, D // TILE, second, 0)
        for j in (3, 2, 1, 0):
            send(
                part.at[g, 4 + j], other.at[g, j], q_send.at[g, j], q_recv.at[g, j], along_z(-1)
            )

    def gather_pair(g):
        for j in (3, 2, 1, 0):
            arrived(other.at[g, j], q_recv.at[g, j])
            value = (part[g, j].astype(F32) + other[g, j].astype(F32)).astype(BF16)
            if j == 0:
                back[g, pair] = value
            else:
                total[g, j] = value
                send(
                    total.at[g, j], back.at[g, pair],
                    t_send.at[g, j], t_recv.at[g, j], along_z(j),
                )

    def give_back(g):
        for slot, step in ((1, 1), (2, -2), (3, 3)):
            arrived(back.at[g, lax.div(along_z(step), 2)], t_recv.at[g, slot])
        for n in range(D // TILE):
            cols = pl.ds(n * TILE, TILE)
            xb[g, :, :, cols] = (
                lax.dot_general(
                    pairs[...], back[g, :, :, cols].reshape(128, TILE),
                    (((0,), (0,)), ((), ())), preferred_element_type=F32,
                )
                .astype(BF16)
                .reshape(ROWS, 16, TILE)
            )
        yy = along_y(-step_along_y(g))
        for i in range(ROWS):
            s = lax.rem(me + i, ROWS)

            def start_remote(s=s):
                pltpu.make_async_remote_copy(
                    xb.at[g, s], out_h.at[y, me], xb_send.at[g], xb_recv.at[g],
                    device_id=at(s, yy, z), device_id_type=MESH,
                ).start()

            if i:
                start_remote()
            else:

                @pl.when(g == 0)
                def _():
                    pltpu.make_async_copy(xb.at[g, me], out_h.at[y, me], xb_recv.at[g]).start()

                pl.when(g > 0)(start_remote)

    stages = (dispatch, forward, experts, gather_pair, give_back)

    def turn(t, carry):
        for lag, stage in enumerate(stages):
            g = t - lag
            pl.when(jnp.logical_and(g >= 0, g < GROUPS))(functools.partial(stage, g))
        return carry

    lax.fori_loop(0, GROUPS + len(stages) - 1, turn, 0)

    spread_out.wait()
    for g in range(GROUPS):
        first_row = 1 if g == 0 else 0
        remote = pl.ds(first_row, ROWS - first_row)
        arrived(slots.at[g, remote], xa_send.at[g])
        for slot in range(4):
            arrived(za.at[g, slot], z_send.at[g, slot])
            arrived(part.at[g, 4 + slot], q_send.at[g, slot])
            if slot:
                arrived(rows.at[g, slot], f_send.at[g, slot])
                arrived(total.at[g, slot], t_send.at[g, slot])
        arrived(xb.at[g, remote], xb_send.at[g])
        arrived(out_h.at[along_y((0, 1, 3, 2)[g])], xb_recv.at[g])


def exchange(images, router, w_in, w_out, words):
    order = jnp.asarray(slot_order(), BF16)
    pairs = jnp.asarray(pair_order(), BF16)
    bits = jnp.asarray(bit_table(), BF16)
    anywhere = pl.BlockSpec(memory_space=pl.ANY)
    dma = pltpu.SemaphoreType.DMA
    return pl.pallas_call(
        kernel,
        out_shape=(
            jax.ShapeDtypeStruct((GROUPS, ROWS, 16, D), BF16),
            jax.ShapeDtypeStruct((IMG * PATCHES, IMG * E), BF16),
        ),
        in_specs=[anywhere] * 8,
        out_specs=(anywhere, anywhere),
        scratch_shapes=[
            pltpu.VMEM((IMG, PATCHES, D), BF16),
            pltpu.VMEM((D, E), BF16),
            pltpu.VMEM((D, D), BF16),
            pltpu.VMEM((D, D), BF16),
            pltpu.VMEM((IMAGES, 128), jnp.int32),
            pltpu.VMEM((512, 512), BF16),
            pltpu.VMEM((128, 128), BF16),
            pltpu.VMEM((256, D), BF16),
            pltpu.VMEM((IMAGES, 256), BF16),
            pltpu.VMEM((IMG, PATCHES, E), F32),
            pltpu.VMEM((IMG * E, D), BF16),
            pltpu.VMEM((GROUPS, ROWS, 16, D), BF16),
            pltpu.VMEM((GROUPS, ROWS, 16, D), BF16),
            pltpu.VMEM((GROUPS, PAIRS, 32, D), BF16),
            pltpu.VMEM((GROUPS, 8, 32, D), BF16),
            pltpu.VMEM((GROUPS, 8, 32, D), BF16),
            pltpu.VMEM((GROUPS, 4, 32, D), BF16),
            pltpu.VMEM((GROUPS, 4, 32, D), BF16),
            pltpu.VMEM((GROUPS, PAIRS, 32, D), BF16),
            pltpu.VMEM((GROUPS, ROWS, 16, D), BF16),
            pltpu.VMEM((256, D), BF16),
            pltpu.VMEM((256, D), BF16),
            pltpu.VMEM((IMG * PATCHES, IMG * E), BF16),
            dma((11,)),
            dma((4,)), dma((4,)),
            dma((4, 4)), dma((4, 4)),
            dma((4, 4)), dma((4, 4)),
            dma((4, 4)), dma((4, 4)),
            dma((4, 4)), dma((4, 4)),
            dma((4,)), dma((4,)),
            dma,
        ],
        compiler_params=pltpu.CompilerParams(
            collective_id=0, has_side_effects=True, vmem_limit_bytes=60 * 2**20
        ),
    )(images, router, w_in, w_out, words, order, pairs, bits)


def on_device(images, router, w_in, w_out, keep_bits):
    words = keep_bits.reshape(IMAGES, 128)
    arrived, spread = exchange(images, router, w_in, w_out, words)
    mixed = jnp.dot(spread, arrived.reshape(512, D), preferred_element_type=F32)
    return mixed.astype(BF16).reshape(IMG, PATCHES, D)


def solution(mesh):
    placed = (
        P(("dp", "expert"), None, None),
        P(),
        P(("dp", "expert"), None, None),
        P(("dp", "expert"), None, None),
        P(None, ("dp", "expert"), None),
    )
    return jax.shard_map(
        on_device,
        mesh=mesh,
        in_specs=placed,
        out_specs=P(("dp", "expert"), None, None),
        check_vma=False,
    )
```

```python
import functools

import jax
import jax.numpy as jnp
import numpy as np
from jax import lax
from jax.experimental import pallas as pl
from jax.experimental.pallas import tpu as pltpu
from jax.sharding import PartitionSpec as P

GROUPS = 8
PLANE = 32
UNITS = 4
OFFSETS = (
    (0, 0), (1, 0), (0, 1), (1, 1), (2, 0), (1, 3), (2, 2), (0, 2),
    (2, 1), (2, 3), (1, 2), (3, 2), (3, 1), (3, 3), (3, 0), (0, 3),
)
PAIRS = 4
IMG = 4
PATCHES = 256
D = 1280
E = 128
IMAGES = 1024
TILE = 256
MESH = pl.DeviceIdType.MESH
KEEP_RATE = 0.875
BF16 = jnp.bfloat16
F32 = jnp.float32


def slot_order():
    table = np.zeros((PLANE * PAIRS * IMG, IMG * E), np.float32)
    for s in range(PLANE):
        for q in range(PAIRS):
            local = (s // 8) * 16 + (s % 2) * 8 + (s // 2 % 4) * 2
            expert = (q // 2) * 64 + local + q % 2
            for b in range(IMG):
                table[(s * PAIRS + q) * IMG + b, b * E + expert] = 1.0
    return table


def pair_order():
    table = np.zeros((64, 64), np.float32)
    for q in range(PAIRS):
        for u in range(UNITS):
            for b in range(IMG):
                table[(q * UNITS + u) * IMG + b, (u * PAIRS + q) * IMG + b] = 1.0
    return table


def bit_table():
    table = np.zeros((256, D), np.float32)
    for w in range(128):
        for i in range(10):
            table[w, 10 * w + i] = 32.0 / 2**i
            table[128 + w, 10 * w + i] = 1.0 / 2**i
    return table


def offset(g, chip):
    if isinstance(g, int):
        return OFFSETS[2 * g + chip]
    dx, dy = OFFSETS[chip]
    for i in range(1, GROUPS):
        here = g == i
        dx = jnp.where(here, OFFSETS[2 * i + chip][0], dx)
        dy = jnp.where(here, OFFSETS[2 * i + chip][1], dy)
    return dx, dy


def kernel(
    img_h, router_h, w1_h, w2_h, kb_h, order_h, pairs_h, bits_h,
    out_h, spread_h,
    img, router, w1, w2, kb, order, pairs, bits, words, logits, raw, slots,
    xa, za, rows, part, other, total, back, xb, hidden, keep, spread,
    load_sem, xa_send, xa_recv, z_send, z_recv, f_send, f_recv,
    q_send, q_recv, t_send, t_recv, xb_send, xb_recv, out_sem,
):
    dp = lax.axis_index("dp")
    ex = lax.axis_index("expert")
    core = lax.rem(dp, 2)
    y = lax.rem(lax.div(dp, 2), 4)
    z = lax.div(dp, 8) * 4 + lax.rem(ex, 4)
    x = lax.div(ex, 4)
    me = (y * 4 + x) * 2 + core
    pair = lax.div(z, 2)
    sg = 2 * lax.rem(z, 2) - 1

    def at(s, zz):
        return (
            lax.div(zz, 4) * 8 + lax.div(s, 8) * 2 + lax.rem(s, 2),
            lax.rem(lax.div(s, 2), 4) * 4 + lax.rem(zz, 4),
        )

    def along_z(step):
        return lax.rem(z + step * sg + 8, 8)

    def chip_at(g, chip, sign):
        dx, dy = offset(g, chip)
        return lax.rem(y + sign * dy + 4, 4) * 4 + lax.rem(x + sign * dx + 4, 4)

    def device_at(g, unit, sign):
        side = core if unit % 2 == 0 else 1 - core
        return chip_at(g, unit // 2, sign) * 2 + side

    loads = [
        (img_h.at[0], img.at[0]),
        (router_h, router),
        (img_h.at[1], img.at[1]),
        (img_h.at[2], img.at[2]),
        (img_h.at[3], img.at[3]),
        (order_h, order),
        (pairs_h, pairs),
        (kb_h, kb),
        (bits_h, bits),
        (w1_h.at[0], w1),
        (w2_h.at[0], w2),
    ]
    copies = [
        pltpu.make_async_copy(src, dst, load_sem.at[i]) for i, (src, dst) in enumerate(loads)
    ]
    for copy in copies:
        copy.start()

    barrier = pltpu.get_barrier_semaphore()
    partners = []
    for g in range(GROUPS):
        for u in range(UNITS):
            if g or u:
                partners.append(at(device_at(g, u, 1), z))
    for step in (1, 2, 3, -1, -2):
        partners.append(at(me, along_z(step)))
    for partner in partners:
        pl.semaphore_signal(barrier, inc=1, device_id=partner, device_id_type=MESH)

    for b in range(IMG):
        if b == 0:
            copies[0].wait()
            copies[1].wait()
        else:
            copies[1 + b].wait()
        scores = jnp.dot(img[b], router[...], preferred_element_type=F32)
        logits[b] = scores
        top = jnp.max(scores, axis=0, keepdims=True)
        grown = jnp.exp(scores - top)
        share = (grown / jnp.sum(grown, axis=0, keepdims=True)).astype(BF16)
        for n in range(D // TILE):
            cols = pl.ds(n * TILE, TILE)
            raw[pl.ds(b * E, E), cols] = lax.dot_general(
                share, img[b, :, cols], (((0,), (0,)), ((), ())), preferred_element_type=F32
            ).astype(BF16)

    copies[5].wait()
    for n in range(D // TILE):
        cols = pl.ds(n * TILE, TILE)
        slots[:, :, cols] = (
            jnp.dot(order[...], raw[:, cols], preferred_element_type=F32)
            .astype(BF16)
            .reshape(PLANE, 16, TILE)
        )
    pl.semaphore_wait(barrier, len(partners))
    for g in range(GROUPS):
        for u in range(UNITS):
            s = device_at(g, u, 1)
            land = xa.at[g, (u // 2) * 2 + core]
            if g == 0 and u == 0:
                pltpu.make_async_copy(slots.at[s], land, xa_recv.at[g]).start()
            else:
                pltpu.make_async_remote_copy(
                    slots.at[s], land, xa_send.at[g], xa_recv.at[g],
                    device_id=at(s, z), device_id_type=MESH,
                ).start()

    for b in range(IMG):
        scores = logits[b]
        grown = jnp.exp(scores - jnp.max(scores, axis=1, keepdims=True))
        share = (grown / jnp.sum(grown, axis=1, keepdims=True)).astype(BF16)
        spread[pl.ds(b * PATCHES, PATCHES), :] = lax.dot_general(
            share, order[:, pl.ds(b * E, E)], (((1,), (1,)), ((), ())), preferred_element_type=F32
        ).astype(BF16)
    spread_out = pltpu.make_async_copy(spread, spread_h, out_sem)
    spread_out.start()

    copies[7].wait()
    words[:, pl.ds(0, 128)] = jnp.right_shift(kb[...], 5).astype(F32).astype(BF16)
    words[:, pl.ds(128, 128)] = jnp.bitwise_and(kb[...], 31).astype(F32).astype(BF16)
    for i in (6, 8, 9, 10):
        copies[i].wait()

    def arrived(ref, sem):
        pltpu.make_async_copy(ref, ref, sem).wait()

    def send(src, dst, send_sem, recv_sem, zz):
        pltpu.make_async_remote_copy(
            src, dst, send_sem, recv_sem, device_id=at(me, zz), device_id_type=MESH
        ).start()

    def dispatch(g):
        arrived(xa.at[g], xa_recv.at[g])
        for n in range(D // TILE):
            cols = pl.ds(n * TILE, TILE)
            za[g, :, :, cols] = (
                jnp.dot(
                    pairs[...], xa[g, :, :, cols].reshape(64, TILE), preferred_element_type=F32
                )
                .astype(BF16)
                .reshape(PAIRS, 16, TILE)
            )
        send(za.at[g, pair], rows.at[g, 4], z_send.at[g, 0], z_recv.at[g, 0], along_z(-1))
        for slot, step in ((3, 3), (2, -2), (1, 1)):
            zz = along_z(step)
            send(
                za.at[g, lax.div(zz, 2)], rows.at[g, slot],
                z_send.at[g, slot], z_recv.at[g, slot], zz,
            )
        rows[g, 0] = za[g, pair]

    def keep_flags(g):
        r = lax.broadcasted_iota(jnp.int32, (128, 1), 0)
        j = jnp.right_shift(r, 4)
        side = jnp.bitwise_and(jnp.right_shift(r, 2), 1)
        zz = jnp.bitwise_and(jnp.where(j < 4, z + j * sg, z - (j - 3) * sg) + 8, 7)
        near, far = chip_at(g, 0, -1), chip_at(g, 1, -1)
        chip = jnp.where(jnp.bitwise_and(r, 8) == 0, near, far)
        group = jnp.right_shift(zz, 2) * 8 + jnp.right_shift(chip, 2) * 2 + side
        device = group * 16 + jnp.bitwise_and(chip, 3) * 4 + jnp.bitwise_and(zz, 3)
        image = device * IMG + jnp.bitwise_and(r, 3)
        c = lax.broadcasted_iota(jnp.int32, (128, IMAGES), 1)
        pick = jnp.where(c == image, 1.0, 0.0).astype(BF16)
        mine = jnp.dot(pick, words[...], preferred_element_type=F32).astype(BF16)

        def tile(n, carry):
            cols = pl.ds(pl.multiple_of(n * TILE, TILE), TILE)
            value = jnp.dot(mine, bits[:, cols], preferred_element_type=F32)
            flag = jnp.bitwise_and(value.astype(jnp.int32), 1)
            keep[:, cols] = flag.astype(F32).astype(BF16)
            return carry

        lax.fori_loop(0, D // TILE, tile, 0)

    def forward(g):
        for j in (3, 2, 1):
            arrived(rows.at[g, j], z_recv.at[g, j])
            send(
                rows.at[g, j], rows.at[g, 4 + j], f_send.at[g, j], f_recv.at[g, j], along_z(-1)
            )

    def experts(g):
        keep_flags(g)
        arrived(rows.at[g, 4], z_recv.at[g, 0])
        for j in (1, 2, 3):
            arrived(rows.at[g, 4 + j], f_recv.at[g, j])

        def first(n, carry):
            cols = pl.ds(pl.multiple_of(n * TILE, TILE), TILE)
            value = jnp.dot(rows[g].reshape(128, D), w1[:, cols], preferred_element_type=F32)
            flag = keep[:, cols].astype(F32)
            hidden[:, cols] = (jax.nn.gelu(value) * flag * (1.0 / KEEP_RATE)).astype(BF16)
            return carry

        def second(n, carry):
            cols = pl.ds(pl.multiple_of(n * TILE, TILE), TILE)
            value = jnp.dot(hidden[...], w2[:, cols], preferred_element_type=F32)
            part[g, :, :, cols] = value.astype(BF16).reshape(8, 16, TILE)
            return carry

        lax.fori_loop(0, D // TILE, first, 0)
        lax.fori_loop(0, D // TILE, second, 0)
        for j in (3, 2, 1, 0):
            send(
                part.at[g, 4 + j], other.at[g, j], q_send.at[g, j], q_recv.at[g, j], along_z(-1)
            )

    def gather_pair(g):
        for j in (3, 2, 1, 0):
            arrived(other.at[g, j], q_recv.at[g, j])
            value = (part[g, j].astype(F32) + other[g, j].astype(F32)).astype(BF16)
            if j == 0:
                back[g, pair] = value
            else:
                total[g, j] = value
                send(
                    total.at[g, j], back.at[g, pair],
                    t_send.at[g, j], t_recv.at[g, j], along_z(j),
                )

    def give_back(g):
        for slot, step in ((1, 1), (2, -2), (3, 3)):
            arrived(back.at[g, lax.div(along_z(step), 2)], t_recv.at[g, slot])
        for n in range(D // TILE):
            cols = pl.ds(n * TILE, TILE)
            xb[g, :, :, cols] = (
                lax.dot_general(
                    pairs[...], back[g, :, :, cols].reshape(64, TILE),
                    (((0,), (0,)), ((), ())), preferred_element_type=F32,
                )
                .astype(BF16)
                .reshape(UNITS, 16, TILE)
            )
        for u in range(UNITS):
            s = device_at(g, u, -1)
            gone = xb.at[g, (u // 2) * 2 + (core if u % 2 == 0 else 1 - core)]
            land = xb_recv.at[g, u // 2]

            def start_remote(s=s, gone=gone, land=land):
                pltpu.make_async_remote_copy(
                    gone, out_h.at[me], xb_send.at[g], land,
                    device_id=at(s, z), device_id_type=MESH,
                ).start()

            if u:
                start_remote()
            else:

                @pl.when(g == 0)
                def _(gone=gone, land=land):
                    pltpu.make_async_copy(gone, out_h.at[me], land).start()

                pl.when(g > 0)(start_remote)

    stages = (dispatch, forward, experts, gather_pair, give_back)

    def turn(t, carry):
        for lag, stage in enumerate(stages):
            g = t - lag
            pl.when(jnp.logical_and(g >= 0, g < GROUPS))(functools.partial(stage, g))
        return carry

    lax.fori_loop(0, GROUPS + len(stages) - 1, turn, 0)

    spread_out.wait()
    for g in range(GROUPS):
        remote = pl.ds(1, UNITS - 1) if g == 0 else pl.ds(0, UNITS)
        arrived(xa.at[g, remote], xa_send.at[g])
        for slot in range(4):
            arrived(za.at[g, slot], z_send.at[g, slot])
            arrived(part.at[g, 4 + slot], q_send.at[g, slot])
            if slot:
                arrived(rows.at[g, slot], f_send.at[g, slot])
                arrived(total.at[g, slot], t_send.at[g, slot])
        arrived(xb.at[g, remote], xb_send.at[g])
        for chip in range(2):
            arrived(out_h.at[pl.ds(chip_at(g, chip, 1) * 2, 2)], xb_recv.at[g, chip])


def exchange(images, router, w_in, w_out, words):
    order = jnp.asarray(slot_order(), BF16)
    pairs = jnp.asarray(pair_order(), BF16)
    bits = jnp.asarray(bit_table(), BF16)
    anywhere = pl.BlockSpec(memory_space=pl.ANY)
    dma = pltpu.SemaphoreType.DMA
    return pl.pallas_call(
        kernel,
        out_shape=(
            jax.ShapeDtypeStruct((PLANE, 16, D), BF16),
            jax.ShapeDtypeStruct((IMG * PATCHES, IMG * E), BF16),
        ),
        in_specs=[anywhere] * 8,
        out_specs=(anywhere, anywhere),
        scratch_shapes=[
            pltpu.VMEM((IMG, PATCHES, D), BF16),
            pltpu.VMEM((D, E), BF16),
            pltpu.VMEM((D, D), BF16),
            pltpu.VMEM((D, D), BF16),
            pltpu.VMEM((IMAGES, 128), jnp.int32),
            pltpu.VMEM((512, 512), BF16),
            pltpu.VMEM((64, 64), BF16),
            pltpu.VMEM((256, D), BF16),
            pltpu.VMEM((IMAGES, 256), BF16),
            pltpu.VMEM((IMG, PATCHES, E), F32),
            pltpu.VMEM((IMG * E, D), BF16),
            pltpu.VMEM((PLANE, 16, D), BF16),
            pltpu.VMEM((GROUPS, UNITS, 16, D), BF16),
            pltpu.VMEM((GROUPS, PAIRS, 16, D), BF16),
            pltpu.VMEM((GROUPS, 8, 16, D), BF16),
            pltpu.VMEM((GROUPS, 8, 16, D), BF16),
            pltpu.VMEM((GROUPS, 4, 16, D), BF16),
            pltpu.VMEM((GROUPS, 4, 16, D), BF16),
            pltpu.VMEM((GROUPS, PAIRS, 16, D), BF16),
            pltpu.VMEM((GROUPS, UNITS, 16, D), BF16),
            pltpu.VMEM((128, D), BF16),
            pltpu.VMEM((128, D), BF16),
            pltpu.VMEM((IMG * PATCHES, IMG * E), BF16),
            dma((11,)),
            dma((GROUPS,)), dma((GROUPS,)),
            dma((GROUPS, 4)), dma((GROUPS, 4)),
            dma((GROUPS, 4)), dma((GROUPS, 4)),
            dma((GROUPS, 4)), dma((GROUPS, 4)),
            dma((GROUPS, 4)), dma((GROUPS, 4)),
            dma((GROUPS,)), dma((GROUPS, 2)),
            dma,
        ],
        compiler_params=pltpu.CompilerParams(
            collective_id=0, has_side_effects=True, vmem_limit_bytes=60 * 2**20
        ),
    )(images, router, w_in, w_out, words, order, pairs, bits)


def on_device(images, router, w_in, w_out, keep_bits):
    words = keep_bits.reshape(IMAGES, 128)
    arrived, spread = exchange(images, router, w_in, w_out, words)
    mixed = jnp.dot(spread, arrived.reshape(512, D), preferred_element_type=F32)
    return mixed.astype(BF16).reshape(IMG, PATCHES, D)


def solution(mesh):
    placed = (
        P(("dp", "expert"), None, None),
        P(),
        P(("dp", "expert"), None, None),
        P(("dp", "expert"), None, None),
        P(None, ("dp", "expert"), None),
    )
    return jax.shard_map(
        on_device,
        mesh=mesh,
        in_specs=placed,
        out_specs=P(("dp", "expert"), None, None),
        check_vma=False,
    )
```

```python
import functools

import jax
import jax.numpy as jnp
import numpy as np
from jax import lax
from jax.experimental import pallas as pl
from jax.experimental.pallas import tpu as pltpu
from jax.sharding import PartitionSpec as P

GROUPS = 8
PLANE = 32
UNITS = 4
AHEAD = 2
OFFSETS = (
    (0, 0), (1, 0), (0, 1), (1, 1), (2, 0), (0, 2), (2, 1), (2, 3),
    (1, 2), (3, 2), (2, 2), (3, 3), (1, 3), (3, 1), (3, 0), (0, 3),
)
PAIRS = 4
IMG = 4
PATCHES = 256
D = 1280
E = 128
IMAGES = 1024
TILE = 256
MESH = pl.DeviceIdType.MESH
KEEP_RATE = 0.875
BF16 = jnp.bfloat16
F32 = jnp.float32


def slot_order():
    table = np.zeros((PLANE * PAIRS * IMG, IMG * E), np.float32)
    for s in range(PLANE):
        for q in range(PAIRS):
            local = (s // 8) * 16 + (s % 2) * 8 + (s // 2 % 4) * 2
            expert = (q // 2) * 64 + local + q % 2
            for b in range(IMG):
                table[(s * PAIRS + q) * IMG + b, b * E + expert] = 1.0
    return table


def pair_order():
    table = np.zeros((64, 64), np.float32)
    for q in range(PAIRS):
        for u in range(UNITS):
            for b in range(IMG):
                table[(q * UNITS + u) * IMG + b, (u * PAIRS + q) * IMG + b] = 1.0
    return table


def bit_table():
    table = np.zeros((256, D), np.float32)
    for w in range(128):
        for i in range(10):
            table[w, 10 * w + i] = 32.0 / 2**i
            table[128 + w, 10 * w + i] = 1.0 / 2**i
    return table


def offset(g, chip):
    if isinstance(g, int):
        return OFFSETS[2 * g + chip]
    dx, dy = OFFSETS[chip]
    for i in range(1, GROUPS):
        here = g == i
        dx = jnp.where(here, OFFSETS[2 * i + chip][0], dx)
        dy = jnp.where(here, OFFSETS[2 * i + chip][1], dy)
    return dx, dy


def kernel(
    img_h, router_h, w1_h, w2_h, kb_h, order_h, pairs_h, bits_h,
    out_h, spread_h,
    img, router, w1, w2, kb, order, pairs, bits, words, logits, raw, slots,
    xa, za, rows, part, other, total, back, xb, hidden, keep, spread,
    load_sem, xa_send, xa_recv, z_send, z_recv, f_send, f_recv,
    q_send, q_recv, t_send, t_recv, xb_send, xb_recv, out_sem,
):
    dp = lax.axis_index("dp")
    ex = lax.axis_index("expert")
    core = lax.rem(dp, 2)
    y = lax.rem(lax.div(dp, 2), 4)
    z = lax.div(dp, 8) * 4 + lax.rem(ex, 4)
    x = lax.div(ex, 4)
    me = (y * 4 + x) * 2 + core
    pair = lax.div(z, 2)
    sg = 2 * lax.rem(z, 2) - 1

    def at(s, zz):
        return (
            lax.div(zz, 4) * 8 + lax.div(s, 8) * 2 + lax.rem(s, 2),
            lax.rem(lax.div(s, 2), 4) * 4 + lax.rem(zz, 4),
        )

    def along_z(step):
        return lax.rem(z + step * sg + 8, 8)

    def chip_at(g, chip, sign):
        dx, dy = offset(g, chip)
        return lax.rem(y + sign * dy + 4, 4) * 4 + lax.rem(x + sign * dx + 4, 4)

    def device_at(g, unit, sign):
        side = core if unit % 2 == 0 else 1 - core
        return chip_at(g, unit // 2, sign) * 2 + side

    loads = [
        (img_h.at[0], img.at[0]),
        (router_h, router),
        (img_h.at[1], img.at[1]),
        (img_h.at[2], img.at[2]),
        (img_h.at[3], img.at[3]),
        (order_h, order),
        (pairs_h, pairs),
        (kb_h, kb),
        (bits_h, bits),
        (w1_h.at[0], w1),
        (w2_h.at[0], w2),
    ]
    copies = [
        pltpu.make_async_copy(src, dst, load_sem.at[i]) for i, (src, dst) in enumerate(loads)
    ]
    for copy in copies:
        copy.start()

    barrier = pltpu.get_barrier_semaphore()
    partners = []
    for g in range(GROUPS):
        for u in range(UNITS):
            if g or u:
                partners.append(at(device_at(g, u, 1), z))
    for step in (1, 2, 3, -1, -2):
        partners.append(at(me, along_z(step)))
    for partner in partners:
        pl.semaphore_signal(barrier, inc=1, device_id=partner, device_id_type=MESH)

    for b in range(IMG):
        if b == 0:
            copies[0].wait()
            copies[1].wait()
        else:
            copies[1 + b].wait()
        scores = jnp.dot(img[b], router[...], preferred_element_type=F32)
        logits[b] = scores
        top = jnp.max(scores, axis=0, keepdims=True)
        grown = jnp.exp(scores - top)
        share = (grown / jnp.sum(grown, axis=0, keepdims=True)).astype(BF16)
        for n in range(D // TILE):
            cols = pl.ds(n * TILE, TILE)
            raw[pl.ds(b * E, E), cols] = lax.dot_general(
                share, img[b, :, cols], (((0,), (0,)), ((), ())), preferred_element_type=F32
            ).astype(BF16)

    copies[5].wait()
    for n in range(D // TILE):
        cols = pl.ds(n * TILE, TILE)
        slots[:, :, cols] = (
            jnp.dot(order[...], raw[:, cols], preferred_element_type=F32)
            .astype(BF16)
            .reshape(PLANE, 16, TILE)
        )
    pl.semaphore_wait(barrier, len(partners))

    def send_plane(g):
        for u in range(UNITS):
            s = device_at(g, u, 1)
            land = xa.at[g, (u // 2) * 2 + core]
            if isinstance(g, int) and g == 0 and u == 0:
                pltpu.make_async_copy(slots.at[s], land, xa_recv.at[g]).start()
            else:
                pltpu.make_async_remote_copy(
                    slots.at[s], land, xa_send, xa_recv.at[g],
                    device_id=at(s, z), device_id_type=MESH,
                ).start()

    for g in range(AHEAD):
        send_plane(g)

    for b in range(IMG):
        scores = logits[b]
        grown = jnp.exp(scores - jnp.max(scores, axis=1, keepdims=True))
        share = (grown / jnp.sum(grown, axis=1, keepdims=True)).astype(BF16)
        spread[pl.ds(b * PATCHES, PATCHES), :] = lax.dot_general(
            share, order[:, pl.ds(b * E, E)], (((1,), (1,)), ((), ())), preferred_element_type=F32
        ).astype(BF16)
    spread_out = pltpu.make_async_copy(spread, spread_h, out_sem)
    spread_out.start()

    copies[7].wait()
    words[:, pl.ds(0, 128)] = jnp.right_shift(kb[...], 5).astype(F32).astype(BF16)
    words[:, pl.ds(128, 128)] = jnp.bitwise_and(kb[...], 31).astype(F32).astype(BF16)
    for i in (6, 8, 9, 10):
        copies[i].wait()

    def arrived(ref, sem):
        pltpu.make_async_copy(ref, ref, sem).wait()

    def send(src, dst, send_sem, recv_sem, zz):
        pltpu.make_async_remote_copy(
            src, dst, send_sem, recv_sem, device_id=at(me, zz), device_id_type=MESH
        ).start()

    def dispatch(g):
        pl.when(g + AHEAD < GROUPS)(functools.partial(send_plane, g + AHEAD))
        arrived(xa.at[g], xa_recv.at[g])
        for n in range(D // TILE):
            cols = pl.ds(n * TILE, TILE)
            za[g, :, :, cols] = (
                jnp.dot(
                    pairs[...], xa[g, :, :, cols].reshape(64, TILE), preferred_element_type=F32
                )
                .astype(BF16)
                .reshape(PAIRS, 16, TILE)
            )
        send(za.at[g, pair], rows.at[g, 4], z_send, f_recv.at[g], along_z(-1))
        for slot, step in ((3, 3), (2, -2), (1, 1)):
            zz = along_z(step)
            send(
                za.at[g, lax.div(zz, 2)], rows.at[g, slot],
                z_send, z_recv.at[g, slot - 1], zz,
            )
        rows[g, 0] = za[g, pair]

    def keep_flags(g):
        r = lax.broadcasted_iota(jnp.int32, (128, 1), 0)
        j = jnp.right_shift(r, 4)
        side = jnp.bitwise_and(jnp.right_shift(r, 2), 1)
        zz = jnp.bitwise_and(jnp.where(j < 4, z + j * sg, z - (j - 3) * sg) + 8, 7)
        near, far = chip_at(g, 0, -1), chip_at(g, 1, -1)
        chip = jnp.where(jnp.bitwise_and(r, 8) == 0, near, far)
        group = jnp.right_shift(zz, 2) * 8 + jnp.right_shift(chip, 2) * 2 + side
        device = group * 16 + jnp.bitwise_and(chip, 3) * 4 + jnp.bitwise_and(zz, 3)
        image = device * IMG + jnp.bitwise_and(r, 3)
        c = lax.broadcasted_iota(jnp.int32, (128, IMAGES), 1)
        pick = jnp.where(c == image, 1.0, 0.0).astype(BF16)
        mine = jnp.dot(pick, words[...], preferred_element_type=F32).astype(BF16)

        def tile(n, carry):
            cols = pl.ds(pl.multiple_of(n * TILE, TILE), TILE)
            value = jnp.dot(mine, bits[:, cols], preferred_element_type=F32)
            flag = jnp.bitwise_and(value.astype(jnp.int32), 1)
            keep[:, cols] = flag.astype(F32).astype(BF16)
            return carry

        lax.fori_loop(0, D // TILE, tile, 0)

    def forward(g):
        for j in (3, 2, 1):
            arrived(rows.at[g, j], z_recv.at[g, j - 1])
            send(rows.at[g, j], rows.at[g, 4 + j], f_send, f_recv.at[g], along_z(-1))

    def experts(g):
        keep_flags(g)
        arrived(rows.at[g, pl.ds(4, 4)], f_recv.at[g])

        def first(n, carry):
            cols = pl.ds(pl.multiple_of(n * TILE, TILE), TILE)
            value = jnp.dot(rows[g].reshape(128, D), w1[:, cols], preferred_element_type=F32)
            flag = keep[:, cols].astype(F32)
            hidden[:, cols] = (jax.nn.gelu(value) * flag * (1.0 / KEEP_RATE)).astype(BF16)
            return carry

        def second(n, carry):
            cols = pl.ds(pl.multiple_of(n * TILE, TILE), TILE)
            value = jnp.dot(hidden[...], w2[:, cols], preferred_element_type=F32)
            part[g, :, :, cols] = value.astype(BF16).reshape(8, 16, TILE)
            return carry

        lax.fori_loop(0, D // TILE, first, 0)
        lax.fori_loop(0, D // TILE, second, 0)
        for half in (1, 0):
            src, dst = part.at[g, pl.ds(4 + 2 * half, 2)], other.at[g, pl.ds(2 * half, 2)]
            send(src, dst, q_send, q_recv.at[g, half], along_z(-1))

    def gather_pair(g):
        for j in (3, 2, 1, 0):
            if j % 2:
                arrived(other.at[g, pl.ds(j - 1, 2)], q_recv.at[g, j // 2])
            value = (part[g, j].astype(F32) + other[g, j].astype(F32)).astype(BF16)
            if j == 0:
                back[g, pair] = value
            else:
                total[g, j] = value
                send(total.at[g, j], back.at[g, pair], t_send, t_recv.at[g], along_z(j))

    def give_back(g):
        arrived(back.at[g, pl.ds(0, 3)], t_recv.at[g])
        for n in range(D // TILE):
            cols = pl.ds(n * TILE, TILE)
            xb[g, :, :, cols] = (
                lax.dot_general(
                    pairs[...], back[g, :, :, cols].reshape(64, TILE),
                    (((0,), (0,)), ((), ())), preferred_element_type=F32,
                )
                .astype(BF16)
                .reshape(UNITS, 16, TILE)
            )
        for u in range(UNITS):
            s = device_at(g, u, -1)
            gone = xb.at[g, (u // 2) * 2 + (core if u % 2 == 0 else 1 - core)]
            land = xb_recv.at[g]

            def start_remote(s=s, gone=gone, land=land):
                pltpu.make_async_remote_copy(
                    gone, out_h.at[me], xb_send, land,
                    device_id=at(s, z), device_id_type=MESH,
                ).start()

            if u:
                start_remote()
            else:

                @pl.when(g == 0)
                def _(gone=gone, land=land):
                    pltpu.make_async_copy(gone, out_h.at[me], land).start()

                pl.when(g > 0)(start_remote)

    stages = (dispatch, forward, experts, gather_pair, give_back)

    def turn(t, carry):
        for lag, stage in enumerate(stages):
            g = t - lag
            pl.when(jnp.logical_and(g >= 0, g < GROUPS))(functools.partial(stage, g))
        return carry

    lax.fori_loop(0, GROUPS + len(stages) - 1, turn, 0)

    spread_out.wait()
    remote = slots.at[pl.ds(0, PLANE - 1)]
    arrived(remote, xa_send)
    arrived(za, z_send)
    arrived(part.at[pl.ds(0, 3)], f_send)
    arrived(other, q_send)
    arrived(part.at[pl.ds(0, 3)], t_send)
    arrived(remote, xb_send)
    for g in range(GROUPS):
        arrived(out_h.at[pl.ds(0, UNITS)], xb_recv.at[g])


def exchange(images, router, w_in, w_out, words):
    order = jnp.asarray(slot_order(), BF16)
    pairs = jnp.asarray(pair_order(), BF16)
    bits = jnp.asarray(bit_table(), BF16)
    anywhere = pl.BlockSpec(memory_space=pl.ANY)
    dma = pltpu.SemaphoreType.DMA
    return pl.pallas_call(
        kernel,
        out_shape=(
            jax.ShapeDtypeStruct((PLANE, 16, D), BF16),
            jax.ShapeDtypeStruct((IMG * PATCHES, IMG * E), BF16),
        ),
        in_specs=[anywhere] * 8,
        out_specs=(anywhere, anywhere),
        scratch_shapes=[
            pltpu.VMEM((IMG, PATCHES, D), BF16),
            pltpu.VMEM((D, E), BF16),
            pltpu.VMEM((D, D), BF16),
            pltpu.VMEM((D, D), BF16),
            pltpu.VMEM((IMAGES, 128), jnp.int32),
            pltpu.VMEM((512, 512), BF16),
            pltpu.VMEM((64, 64), BF16),
            pltpu.VMEM((256, D), BF16),
            pltpu.VMEM((IMAGES, 256), BF16),
            pltpu.VMEM((IMG, PATCHES, E), F32),
            pltpu.VMEM((IMG * E, D), BF16),
            pltpu.VMEM((PLANE, 16, D), BF16),
            pltpu.VMEM((GROUPS, UNITS, 16, D), BF16),
            pltpu.VMEM((GROUPS, PAIRS, 16, D), BF16),
            pltpu.VMEM((GROUPS, 8, 16, D), BF16),
            pltpu.VMEM((GROUPS, 8, 16, D), BF16),
            pltpu.VMEM((GROUPS, 4, 16, D), BF16),
            pltpu.VMEM((GROUPS, 4, 16, D), BF16),
            pltpu.VMEM((GROUPS, PAIRS, 16, D), BF16),
            pltpu.VMEM((GROUPS, UNITS, 16, D), BF16),
            pltpu.VMEM((128, D), BF16),
            pltpu.VMEM((128, D), BF16),
            pltpu.VMEM((IMG * PATCHES, IMG * E), BF16),
            dma((11,)),
            dma, dma((GROUPS,)),
            dma, dma((GROUPS, 3)),
            dma, dma((GROUPS,)),
            dma, dma((GROUPS, 2)),
            dma, dma((GROUPS,)),
            dma, dma((GROUPS,)),
            dma,
        ],
        compiler_params=pltpu.CompilerParams(
            collective_id=0, has_side_effects=True, vmem_limit_bytes=60 * 2**20
        ),
    )(images, router, w_in, w_out, words, order, pairs, bits)


def on_device(images, router, w_in, w_out, keep_bits):
    words = keep_bits.reshape(IMAGES, 128)
    arrived, spread = exchange(images, router, w_in, w_out, words)
    mixed = jnp.dot(spread, arrived.reshape(512, D), preferred_element_type=F32)
    return mixed.astype(BF16).reshape(IMG, PATCHES, D)


def solution(mesh):
    placed = (
        P(("dp", "expert"), None, None),
        P(),
        P(("dp", "expert"), None, None),
        P(("dp", "expert"), None, None),
        P(None, ("dp", "expert"), None),
    )
    return jax.shard_map(
        on_device,
        mesh=mesh,
        in_specs=placed,
        out_specs=P(("dp", "expert"), None, None),
        check_vma=False,
    )
```

```python
import functools

import jax
import jax.numpy as jnp
import numpy as np
from jax import lax
from jax.experimental import pallas as pl
from jax.experimental.pallas import tpu as pltpu
from jax.sharding import PartitionSpec as P

GROUPS = 8
PLANE = 32
UNITS = 4
AHEAD = 2
OFFSETS = (
    (0, 0), (1, 0), (0, 1), (0, 3), (2, 0), (0, 2), (2, 1), (2, 3),
    (1, 2), (3, 2), (2, 2), (3, 3), (1, 3), (3, 1), (3, 0), (1, 1),
)
PAIRS = 4
IMG = 4
PATCHES = 256
D = 1280
E = 128
IMAGES = 1024
TILE = 256
MESH = pl.DeviceIdType.MESH
KEEP_RATE = 0.875
BF16 = jnp.bfloat16
F32 = jnp.float32


def slot_order():
    table = np.zeros((PLANE * PAIRS * IMG, IMG * E), np.float32)
    for s in range(PLANE):
        for q in range(PAIRS):
            local = (s // 8) * 16 + (s % 2) * 8 + (s // 2 % 4) * 2
            expert = (q // 2) * 64 + local + q % 2
            for b in range(IMG):
                table[(s * PAIRS + q) * IMG + b, b * E + expert] = 1.0
    return table


def pair_order():
    table = np.zeros((64, 64), np.float32)
    for q in range(PAIRS):
        for u in range(UNITS):
            for b in range(IMG):
                table[(q * UNITS + u) * IMG + b, (u * PAIRS + q) * IMG + b] = 1.0
    return table


def bit_table():
    table = np.zeros((256, D), np.float32)
    for w in range(128):
        for i in range(10):
            table[w, 10 * w + i] = 32.0 / 2**i
            table[128 + w, 10 * w + i] = 1.0 / 2**i
    return table


def offset(g, chip):
    if isinstance(g, int):
        return OFFSETS[2 * g + chip]
    dx, dy = OFFSETS[chip]
    for i in range(1, GROUPS):
        here = g == i
        dx = jnp.where(here, OFFSETS[2 * i + chip][0], dx)
        dy = jnp.where(here, OFFSETS[2 * i + chip][1], dy)
    return dx, dy


def kernel(
    img_h, router_h, w1_h, w2_h, kb_h, order_h, pairs_h, bits_h,
    out_h, spread_h,
    img, router, w1, w2, kb, order, pairs, bits, words, logits, raw, slots, first_slots,
    xa, za, rows, part, other, total, back, xb, hidden, keep, spread,
    load_sem, xa_send, xa_recv, z_send, z_recv, f_send, f_recv,
    q_send, q_recv, t_send, t_recv, xb_send, xb_recv, out_sem,
):
    dp = lax.axis_index("dp")
    ex = lax.axis_index("expert")
    core = lax.rem(dp, 2)
    y = lax.rem(lax.div(dp, 2), 4)
    z = lax.div(dp, 8) * 4 + lax.rem(ex, 4)
    x = lax.div(ex, 4)
    me = (y * 4 + x) * 2 + core
    pair = lax.div(z, 2)
    sg = 2 * lax.rem(z, 2) - 1

    def at(s, zz):
        return (
            lax.div(zz, 4) * 8 + lax.div(s, 8) * 2 + lax.rem(s, 2),
            lax.rem(lax.div(s, 2), 4) * 4 + lax.rem(zz, 4),
        )

    def along_z(step):
        return lax.rem(z + step * sg + 8, 8)

    def chip_at(g, chip, sign):
        dx, dy = offset(g, chip)
        return lax.rem(y + sign * dy + 4, 4) * 4 + lax.rem(x + sign * dx + 4, 4)

    def device_at(g, unit, sign):
        side = core if unit % 2 == 0 else 1 - core
        return chip_at(g, unit // 2, sign) * 2 + side

    loads = [
        (img_h.at[pl.ds(0, 2)], img.at[pl.ds(0, 2)]),
        (router_h, router),
        (img_h.at[pl.ds(2, 2)], img.at[pl.ds(2, 2)]),
        (order_h, order),
        (pairs_h, pairs),
        (kb_h, kb),
        (bits_h, bits),
        (w1_h.at[0], w1),
        (w2_h.at[0], w2),
    ]
    copies = [
        pltpu.make_async_copy(src, dst, load_sem.at[i]) for i, (src, dst) in enumerate(loads)
    ]
    for copy in copies[:4]:
        copy.start()

    barrier = pltpu.get_barrier_semaphore()
    partners = []
    for g in range(GROUPS):
        for u in range(UNITS):
            if g or u:
                partners.append(at(device_at(g, u, 1), z))
    for step in (1, 2, 3, -1, -2):
        partners.append(at(me, along_z(step)))
    for partner in partners:
        pl.semaphore_signal(barrier, inc=1, device_id=partner, device_id_type=MESH)

    copies[1].wait()
    for half in range(2):
        copies[2 * half].wait()
        both = jnp.dot(
            img[pl.ds(2 * half, 2)].reshape(2 * PATCHES, D), router[...],
            preferred_element_type=F32,
        )
        for b in (2 * half, 2 * half + 1):
            scores = both[(b % 2) * PATCHES : (b % 2 + 1) * PATCHES]
            logits[b] = scores
            top = jnp.max(scores, axis=0, keepdims=True)
            grown = jnp.exp(scores - top)
            share = (grown / jnp.sum(grown, axis=0, keepdims=True)).astype(BF16)
            for n in range(D // TILE):
                cols = pl.ds(n * TILE, TILE)
                raw[pl.ds(b * E, E), cols] = lax.dot_general(
                    share, img[b, :, cols], (((0,), (0,)), ((), ())), preferred_element_type=F32
                ).astype(BF16)

    for copy in copies[4:]:
        copy.start()
    copies[3].wait()
    near = jnp.concatenate(
        [order[pl.ds(pl.multiple_of(chip_at(0, c, 1) * 32, 32), 32), :] for c in range(2)], axis=0
    )
    for n in range(D // TILE):
        cols = pl.ds(n * TILE, TILE)
        first_slots[:, :, cols] = (
            jnp.dot(near, raw[:, cols], preferred_element_type=F32)
            .astype(BF16)
            .reshape(UNITS, 16, TILE)
        )
    pl.semaphore_wait(barrier, len(partners))

    def send_plane(g):
        for u in range(UNITS):
            s = device_at(g, u, 1)
            land = xa.at[g, (u // 2) * 2 + core]
            early = isinstance(g, int) and g == 0
            if early:
                src = first_slots.at[(u // 2) * 2 + lax.rem(s, 2)]
            else:
                src = slots.at[s]
            if early and u == 0:
                pltpu.make_async_copy(src, land, xa_recv.at[g]).start()
            else:
                pltpu.make_async_remote_copy(
                    src, land, xa_send, xa_recv.at[g],
                    device_id=at(s, z), device_id_type=MESH,
                ).start()

    send_plane(0)
    for n in range(D // TILE):
        cols = pl.ds(n * TILE, TILE)
        slots[:, :, cols] = (
            jnp.dot(order[...], raw[:, cols], preferred_element_type=F32)
            .astype(BF16)
            .reshape(PLANE, 16, TILE)
        )
    for g in range(1, AHEAD):
        send_plane(g)

    for b in range(IMG):
        scores = logits[b]
        grown = jnp.exp(scores - jnp.max(scores, axis=1, keepdims=True))
        share = (grown / jnp.sum(grown, axis=1, keepdims=True)).astype(BF16)
        spread[pl.ds(b * PATCHES, PATCHES), :] = lax.dot_general(
            share, order[:, pl.ds(b * E, E)], (((1,), (1,)), ((), ())), preferred_element_type=F32
        ).astype(BF16)
    spread_out = pltpu.make_async_copy(spread, spread_h, out_sem)
    spread_out.start()

    copies[5].wait()
    words[:, pl.ds(0, 128)] = jnp.right_shift(kb[...], 5).astype(F32).astype(BF16)
    words[:, pl.ds(128, 128)] = jnp.bitwise_and(kb[...], 31).astype(F32).astype(BF16)
    for i in (4, 6, 7, 8):
        copies[i].wait()

    def arrived(ref, sem):
        pltpu.make_async_copy(ref, ref, sem).wait()

    def send(src, dst, send_sem, recv_sem, zz):
        pltpu.make_async_remote_copy(
            src, dst, send_sem, recv_sem, device_id=at(me, zz), device_id_type=MESH
        ).start()

    def dispatch(g):
        pl.when(g + AHEAD < GROUPS)(functools.partial(send_plane, g + AHEAD))
        arrived(xa.at[g], xa_recv.at[g])
        for n in range(D // TILE):
            cols = pl.ds(n * TILE, TILE)
            za[g, :, :, cols] = (
                jnp.dot(
                    pairs[...], xa[g, :, :, cols].reshape(64, TILE), preferred_element_type=F32
                )
                .astype(BF16)
                .reshape(PAIRS, 16, TILE)
            )
        send(za.at[g, pair], rows.at[g, 4], z_send, f_recv.at[g], along_z(-1))
        for slot, step in ((3, 3), (2, -2), (1, 1)):
            zz = along_z(step)
            send(
                za.at[g, lax.div(zz, 2)], rows.at[g, slot],
                z_send, z_recv.at[g, slot - 1], zz,
            )
        rows[g, 0] = za[g, pair]

    def keep_flags(g):
        r = lax.broadcasted_iota(jnp.int32, (128, 1), 0)
        j = jnp.right_shift(r, 4)
        side = jnp.bitwise_and(jnp.right_shift(r, 2), 1)
        zz = jnp.bitwise_and(jnp.where(j < 4, z + j * sg, z - (j - 3) * sg) + 8, 7)
        near, far = chip_at(g, 0, -1), chip_at(g, 1, -1)
        chip = jnp.where(jnp.bitwise_and(r, 8) == 0, near, far)
        group = jnp.right_shift(zz, 2) * 8 + jnp.right_shift(chip, 2) * 2 + side
        device = group * 16 + jnp.bitwise_and(chip, 3) * 4 + jnp.bitwise_and(zz, 3)
        image = device * IMG + jnp.bitwise_and(r, 3)
        c = lax.broadcasted_iota(jnp.int32, (128, IMAGES), 1)
        pick = jnp.where(c == image, 1.0, 0.0).astype(BF16)
        mine = jnp.dot(pick, words[...], preferred_element_type=F32).astype(BF16)

        def tile(n, carry):
            cols = pl.ds(pl.multiple_of(n * TILE, TILE), TILE)
            value = jnp.dot(mine, bits[:, cols], preferred_element_type=F32)
            flag = jnp.bitwise_and(value.astype(jnp.int32), 1)
            keep[:, cols] = flag.astype(F32).astype(BF16)
            return carry

        lax.fori_loop(0, D // TILE, tile, 0)

    def forward(g):
        for j in (3, 2, 1):
            arrived(rows.at[g, j], z_recv.at[g, j - 1])
            send(rows.at[g, j], rows.at[g, 4 + j], f_send, f_recv.at[g], along_z(-1))

    def experts(g):
        arrived(rows.at[g, pl.ds(4, 4)], f_recv.at[g])

        def first(n, carry):
            cols = pl.ds(pl.multiple_of(n * TILE, TILE), TILE)
            value = jnp.dot(rows[g].reshape(128, D), w1[:, cols], preferred_element_type=F32)
            flag = keep[:, cols].astype(F32)
            hidden[:, cols] = (jax.nn.gelu(value) * flag * (1.0 / KEEP_RATE)).astype(BF16)
            return carry

        def second(n, carry):
            cols = pl.ds(pl.multiple_of(n * TILE, TILE), TILE)
            value = jnp.dot(hidden[...], w2[:, cols], preferred_element_type=F32)
            part[g, :, :, cols] = value.astype(BF16).reshape(8, 16, TILE)
            return carry

        lax.fori_loop(0, D // TILE, first, 0)
        lax.fori_loop(0, D // TILE, second, 0)
        send(part.at[g, pl.ds(4, 4)], other.at[g], q_send, q_recv.at[g], along_z(-1))
        pl.when(g + 1 < GROUPS)(functools.partial(keep_flags, g + 1))

    def gather_pair(g):
        arrived(other.at[g], q_recv.at[g])
        for j in (3, 2, 1):
            total[g, j] = (part[g, j].astype(F32) + other[g, j].astype(F32)).astype(BF16)
            send(total.at[g, j], back.at[g, pair], t_send, t_recv.at[g], along_z(j))
        back[g, pair] = (part[g, 0].astype(F32) + other[g, 0].astype(F32)).astype(BF16)

    def give_back(g):
        arrived(back.at[g, pl.ds(0, 3)], t_recv.at[g])
        for n in range(D // TILE):
            cols = pl.ds(n * TILE, TILE)
            xb[g, :, :, cols] = (
                lax.dot_general(
                    pairs[...], back[g, :, :, cols].reshape(64, TILE),
                    (((0,), (0,)), ((), ())), preferred_element_type=F32,
                )
                .astype(BF16)
                .reshape(UNITS, 16, TILE)
            )
        for u in range(UNITS):
            s = device_at(g, u, -1)
            gone = xb.at[g, (u // 2) * 2 + (core if u % 2 == 0 else 1 - core)]
            land = xb_recv.at[g]

            def start_remote(s=s, gone=gone, land=land):
                pltpu.make_async_remote_copy(
                    gone, out_h.at[me], xb_send, land,
                    device_id=at(s, z), device_id_type=MESH,
                ).start()

            if u:
                start_remote()
            else:

                @pl.when(g == 0)
                def _(gone=gone, land=land):
                    pltpu.make_async_copy(gone, out_h.at[me], land).start()

                pl.when(g > 0)(start_remote)

    stages = (
        (0, dispatch),
        (1, forward),
        (3, experts),
        (4, gather_pair),
        (5, give_back),
    )

    keep_flags(0)

    def turn(t, carry):
        for lag, stage in stages:
            g = t - lag
            pl.when(jnp.logical_and(g >= 0, g < GROUPS))(functools.partial(stage, g))
        return carry

    lax.fori_loop(0, GROUPS + max(lag for lag, _ in stages), turn, 0)

    spread_out.wait()
    remote = slots.at[pl.ds(0, PLANE - 1)]
    arrived(remote, xa_send)
    arrived(za, z_send)
    arrived(part.at[pl.ds(0, 3)], f_send)
    arrived(other, q_send)
    arrived(part.at[pl.ds(0, 3)], t_send)
    arrived(remote, xb_send)
    for g in range(GROUPS):
        arrived(out_h.at[pl.ds(0, UNITS)], xb_recv.at[g])


def exchange(images, router, w_in, w_out, words):
    order = jnp.asarray(slot_order(), BF16)
    pairs = jnp.asarray(pair_order(), BF16)
    bits = jnp.asarray(bit_table(), BF16)
    anywhere = pl.BlockSpec(memory_space=pl.ANY)
    dma = pltpu.SemaphoreType.DMA
    return pl.pallas_call(
        kernel,
        out_shape=(
            jax.ShapeDtypeStruct((PLANE, 16, D), BF16),
            jax.ShapeDtypeStruct((IMG * PATCHES, IMG * E), BF16),
        ),
        in_specs=[anywhere] * 8,
        out_specs=(anywhere, anywhere),
        scratch_shapes=[
            pltpu.VMEM((IMG, PATCHES, D), BF16),
            pltpu.VMEM((D, E), BF16),
            pltpu.VMEM((D, D), BF16),
            pltpu.VMEM((D, D), BF16),
            pltpu.VMEM((IMAGES, 128), jnp.int32),
            pltpu.VMEM((512, 512), BF16),
            pltpu.VMEM((64, 64), BF16),
            pltpu.VMEM((256, D), BF16),
            pltpu.VMEM((IMAGES, 256), BF16),
            pltpu.VMEM((IMG, PATCHES, E), F32),
            pltpu.VMEM((IMG * E, D), BF16),
            pltpu.VMEM((PLANE, 16, D), BF16),
            pltpu.VMEM((UNITS, 16, D), BF16),
            pltpu.VMEM((GROUPS, UNITS, 16, D), BF16),
            pltpu.VMEM((GROUPS, PAIRS, 16, D), BF16),
            pltpu.VMEM((GROUPS, 8, 16, D), BF16),
            pltpu.VMEM((GROUPS, 8, 16, D), BF16),
            pltpu.VMEM((GROUPS, 4, 16, D), BF16),
            pltpu.VMEM((GROUPS, 4, 16, D), BF16),
            pltpu.VMEM((GROUPS, PAIRS, 16, D), BF16),
            pltpu.VMEM((GROUPS, UNITS, 16, D), BF16),
            pltpu.VMEM((128, D), BF16),
            pltpu.VMEM((128, D), BF16),
            pltpu.VMEM((IMG * PATCHES, IMG * E), BF16),
            dma((9,)),
            dma, dma((GROUPS,)),
            dma, dma((GROUPS, 3)),
            dma, dma((GROUPS,)),
            dma, dma((GROUPS,)),
            dma, dma((GROUPS,)),
            dma, dma((GROUPS,)),
            dma,
        ],
        compiler_params=pltpu.CompilerParams(
            collective_id=0, has_side_effects=True, vmem_limit_bytes=60 * 2**20
        ),
    )(images, router, w_in, w_out, words, order, pairs, bits)


def on_device(images, router, w_in, w_out, keep_bits):
    words = keep_bits.reshape(IMAGES, 128)
    arrived, spread = exchange(images, router, w_in, w_out, words)
    mixed = jnp.dot(spread, arrived.reshape(512, D), preferred_element_type=F32)
    return mixed.astype(BF16).reshape(IMG, PATCHES, D)


def solution(mesh):
    placed = (
        P(("dp", "expert"), None, None),
        P(),
        P(("dp", "expert"), None, None),
        P(("dp", "expert"), None, None),
        P(None, ("dp", "expert"), None),
    )
    return jax.shard_map(
        on_device,
        mesh=mesh,
        in_specs=placed,
        out_specs=P(("dp", "expert"), None, None),
        check_vma=False,
    )
```

```python
import functools

import jax
import jax.numpy as jnp
import numpy as np
from jax import lax
from jax.experimental import pallas as pl
from jax.experimental.pallas import tpu as pltpu
from jax.sharding import PartitionSpec as P

GROUPS = 8
PLANE = 32
UNITS = 4
AHEAD = 2
OFFSETS = (
    (0, 0), (1, 0), (0, 1), (0, 3), (2, 0), (0, 2), (2, 1), (2, 3),
    (1, 2), (3, 2), (2, 2), (3, 3), (1, 3), (3, 1), (3, 0), (1, 1),
)
PAIRS = 4
IMG = 4
PATCHES = 256
D = 1280
E = 128
IMAGES = 1024
TILE = 256
MESH = pl.DeviceIdType.MESH
KEEP_RATE = 0.875
BF16 = jnp.bfloat16
F32 = jnp.float32


def slot_order():
    table = np.zeros((PLANE * PAIRS * IMG, IMG * E), np.float32)
    for s in range(PLANE):
        for q in range(PAIRS):
            local = (s // 8) * 16 + (s % 2) * 8 + (s // 2 % 4) * 2
            expert = (q // 2) * 64 + local + q % 2
            for b in range(IMG):
                table[(s * PAIRS + q) * IMG + b, b * E + expert] = 1.0
    return table


def pair_order():
    table = np.zeros((64, 64), np.float32)
    for q in range(PAIRS):
        for u in range(UNITS):
            for b in range(IMG):
                table[(q * UNITS + u) * IMG + b, (u * PAIRS + q) * IMG + b] = 1.0
    return table


def bit_table():
    table = np.zeros((256, D), np.float32)
    for w in range(128):
        for i in range(10):
            table[w, 10 * w + i] = 32.0 / 2**i
            table[128 + w, 10 * w + i] = 1.0 / 2**i
    return table


def offset(g, chip):
    if isinstance(g, int):
        return OFFSETS[2 * g + chip]
    dx, dy = OFFSETS[chip]
    for i in range(1, GROUPS):
        here = g == i
        dx = jnp.where(here, OFFSETS[2 * i + chip][0], dx)
        dy = jnp.where(here, OFFSETS[2 * i + chip][1], dy)
    return dx, dy


def kernel(
    img_h, router_h, w1_h, w2_h, kb_h, order_h, pairs_h, bits_h,
    out_h, spread_h,
    img, router, w1, w2, kb, order, pairs, bits, words, logits, raw, slots, first_slots,
    xa, za, rows, part, other, total, back, xb, hidden, keep, spread,
    load_sem, xa_send, xa_recv, z_send, z_recv, f_send, f_recv,
    q_send, q_recv, t_send, t_recv, xb_send, xb_recv, out_sem,
):
    dp = lax.axis_index("dp")
    ex = lax.axis_index("expert")
    core = lax.rem(dp, 2)
    y = lax.rem(lax.div(dp, 2), 4)
    z = lax.div(dp, 8) * 4 + lax.rem(ex, 4)
    x = lax.div(ex, 4)
    me = (y * 4 + x) * 2 + core
    pair = lax.div(z, 2)
    sg = 2 * lax.rem(z, 2) - 1

    def at(s, zz):
        return (
            lax.div(zz, 4) * 8 + lax.div(s, 8) * 2 + lax.rem(s, 2),
            lax.rem(lax.div(s, 2), 4) * 4 + lax.rem(zz, 4),
        )

    def along_z(step):
        return lax.rem(z + step * sg + 8, 8)

    def chip_at(g, chip, sign):
        dx, dy = offset(g, chip)
        return lax.rem(y + sign * dy + 4, 4) * 4 + lax.rem(x + sign * dx + 4, 4)

    def device_at(g, unit, sign):
        side = core if unit % 2 == 0 else 1 - core
        return chip_at(g, unit // 2, sign) * 2 + side

    loads = [
        (img_h.at[pl.ds(0, 2)], img.at[pl.ds(0, 2)]),
        (router_h, router),
        (img_h.at[pl.ds(2, 2)], img.at[pl.ds(2, 2)]),
        (order_h, order),
        (pairs_h, pairs),
        (kb_h, kb),
        (bits_h, bits),
        (w1_h.at[0], w1),
        (w2_h.at[0], w2),
    ]
    copies = [
        pltpu.make_async_copy(src, dst, load_sem.at[i]) for i, (src, dst) in enumerate(loads)
    ]
    for copy in copies[:3]:
        copy.start()

    barrier = pltpu.get_barrier_semaphore()
    partners = []
    for g in range(GROUPS):
        for u in range(UNITS):
            if g or u:
                partners.append(at(device_at(g, u, 1), z))
    for step in (1, 2, 3, -1, -2):
        partners.append(at(me, along_z(step)))
    for partner in partners:
        pl.semaphore_signal(barrier, inc=1, device_id=partner, device_id_type=MESH)

    copies[1].wait()
    for half in range(2):
        copies[2 * half].wait()
        if half == 0:
            copies[3].start()
        both = jnp.dot(
            img[pl.ds(2 * half, 2)].reshape(2 * PATCHES, D), router[...],
            preferred_element_type=F32,
        )
        for b in (2 * half, 2 * half + 1):
            scores = both[(b % 2) * PATCHES : (b % 2 + 1) * PATCHES]
            logits[b] = scores
            top = jnp.max(scores, axis=0, keepdims=True)
            grown = jnp.exp(scores - top)
            share = (grown / jnp.sum(grown, axis=0, keepdims=True)).astype(BF16)
            for n in range(D // TILE):
                cols = pl.ds(n * TILE, TILE)
                raw[pl.ds(b * E, E), cols] = lax.dot_general(
                    share, img[b, :, cols], (((0,), (0,)), ((), ())), preferred_element_type=F32
                ).astype(BF16)

    for copy in copies[4:]:
        copy.start()
    copies[3].wait()
    near = jnp.concatenate(
        [order[pl.ds(pl.multiple_of(chip_at(0, c, 1) * 32, 32), 32), :] for c in range(2)], axis=0
    )
    for n in range(D // TILE):
        cols = pl.ds(n * TILE, TILE)
        first_slots[:, :, cols] = (
            jnp.dot(near, raw[:, cols], preferred_element_type=F32)
            .astype(BF16)
            .reshape(UNITS, 16, TILE)
        )
    pl.semaphore_wait(barrier, len(partners))

    def send_plane(g):
        for u in range(UNITS):
            s = device_at(g, u, 1)
            land = xa.at[g, (u // 2) * 2 + core]
            early = isinstance(g, int) and g == 0
            if early:
                src = first_slots.at[(u // 2) * 2 + lax.rem(s, 2)]
            else:
                src = slots.at[s]
            if early and u == 0:
                pltpu.make_async_copy(src, land, xa_recv.at[g]).start()
            else:
                pltpu.make_async_remote_copy(
                    src, land, xa_send, xa_recv.at[g],
                    device_id=at(s, z), device_id_type=MESH,
                ).start()

    send_plane(0)
    for n in range(D // TILE):
        cols = pl.ds(n * TILE, TILE)
        slots[:, :, cols] = (
            jnp.dot(order[...], raw[:, cols], preferred_element_type=F32)
            .astype(BF16)
            .reshape(PLANE, 16, TILE)
        )
    for g in range(1, AHEAD):
        send_plane(g)

    copies[4].wait()

    def arrived(ref, sem):
        pltpu.make_async_copy(ref, ref, sem).wait()

    def send(src, dst, send_sem, recv_sem, zz):
        pltpu.make_async_remote_copy(
            src, dst, send_sem, recv_sem, device_id=at(me, zz), device_id_type=MESH
        ).start()

    def dispatch(g):
        arrived(xa.at[g], xa_recv.at[g])
        for n in range(D // TILE):
            cols = pl.ds(n * TILE, TILE)
            za[g, :, :, cols] = (
                jnp.dot(
                    pairs[...], xa[g, :, :, cols].reshape(64, TILE), preferred_element_type=F32
                )
                .astype(BF16)
                .reshape(PAIRS, 16, TILE)
            )
        send(za.at[g, pair], rows.at[g, 4], z_send, f_recv.at[g], along_z(-1))
        for slot, step in ((3, 3), (2, -2), (1, 1)):
            zz = along_z(step)
            send(
                za.at[g, lax.div(zz, 2)], rows.at[g, slot],
                z_send, z_recv.at[g, slot - 1], zz,
            )
        pl.when(g + AHEAD < GROUPS)(functools.partial(send_plane, g + AHEAD))
        rows[g, 0] = za[g, pair]

    def keep_flags(g):
        r = lax.broadcasted_iota(jnp.int32, (128, 1), 0)
        j = jnp.right_shift(r, 4)
        side = jnp.bitwise_and(jnp.right_shift(r, 2), 1)
        zz = jnp.bitwise_and(jnp.where(j < 4, z + j * sg, z - (j - 3) * sg) + 8, 7)
        near, far = chip_at(g, 0, -1), chip_at(g, 1, -1)
        chip = jnp.where(jnp.bitwise_and(r, 8) == 0, near, far)
        group = jnp.right_shift(zz, 2) * 8 + jnp.right_shift(chip, 2) * 2 + side
        device = group * 16 + jnp.bitwise_and(chip, 3) * 4 + jnp.bitwise_and(zz, 3)
        image = device * IMG + jnp.bitwise_and(r, 3)
        c = lax.broadcasted_iota(jnp.int32, (128, IMAGES), 1)
        pick = jnp.where(c == image, 1.0, 0.0).astype(BF16)
        mine = jnp.dot(pick, words[...], preferred_element_type=F32).astype(BF16)

        def tile(n, carry):
            cols = pl.ds(pl.multiple_of(n * TILE, TILE), TILE)
            value = jnp.dot(mine, bits[:, cols], preferred_element_type=F32)
            flag = jnp.bitwise_and(value.astype(jnp.int32), 1)
            keep[:, cols] = flag.astype(F32).astype(BF16)
            return carry

        lax.fori_loop(0, D // TILE, tile, 0)

    def forward(g):
        for j in (3, 2, 1):
            arrived(rows.at[g, j], z_recv.at[g, j - 1])
            send(rows.at[g, j], rows.at[g, 4 + j], f_send, f_recv.at[g], along_z(-1))

    def experts(g):
        arrived(rows.at[g, pl.ds(4, 4)], f_recv.at[g])

        def first(n, carry):
            cols = pl.ds(pl.multiple_of(n * TILE, TILE), TILE)
            value = jnp.dot(rows[g].reshape(128, D), w1[:, cols], preferred_element_type=F32)
            flag = keep[:, cols].astype(F32)
            hidden[:, cols] = (jax.nn.gelu(value) * flag * (1.0 / KEEP_RATE)).astype(BF16)
            return carry

        def second(n, carry):
            cols = pl.ds(pl.multiple_of(n * TILE, TILE), TILE)
            value = jnp.dot(hidden[...], w2[:, cols], preferred_element_type=F32)
            part[g, :, :, cols] = value.astype(BF16).reshape(8, 16, TILE)
            return carry

        lax.fori_loop(0, D // TILE, first, 0, unroll=True)
        lax.fori_loop(0, D // TILE, second, 0, unroll=True)
        send(part.at[g, pl.ds(4, 4)], other.at[g], q_send, q_recv.at[g], along_z(-1))
        pl.when(g + 1 < GROUPS)(functools.partial(keep_flags, g + 1))

    def gather_pair(g):
        arrived(other.at[g], q_recv.at[g])
        for j in (3, 2, 1):
            total[g, j] = (part[g, j].astype(F32) + other[g, j].astype(F32)).astype(BF16)
            send(total.at[g, j], back.at[g, pair], t_send, t_recv.at[g], along_z(j))
        back[g, pair] = (part[g, 0].astype(F32) + other[g, 0].astype(F32)).astype(BF16)

    def give_back(g):
        arrived(back.at[g, pl.ds(0, 3)], t_recv.at[g])
        for n in range(D // TILE):
            cols = pl.ds(n * TILE, TILE)
            xb[g, :, :, cols] = (
                lax.dot_general(
                    pairs[...], back[g, :, :, cols].reshape(64, TILE),
                    (((0,), (0,)), ((), ())), preferred_element_type=F32,
                )
                .astype(BF16)
                .reshape(UNITS, 16, TILE)
            )
        for u in range(UNITS):
            s = device_at(g, u, -1)
            gone = xb.at[g, (u // 2) * 2 + (core if u % 2 == 0 else 1 - core)]
            land = xb_recv.at[g]

            def start_remote(s=s, gone=gone, land=land):
                pltpu.make_async_remote_copy(
                    gone, out_h.at[me], xb_send, land,
                    device_id=at(s, z), device_id_type=MESH,
                ).start()

            if u:
                start_remote()
            else:

                @pl.when(g == 0)
                def _(gone=gone, land=land):
                    pltpu.make_async_copy(gone, out_h.at[me], land).start()

                pl.when(g > 0)(start_remote)

    stages = (
        (0, dispatch),
        (1, forward),
        (3, experts),
        (4, gather_pair),
        (5, give_back),
    )

    def prepare():
        for b in range(IMG):
            scores = logits[b]
            grown = jnp.exp(scores - jnp.max(scores, axis=1, keepdims=True))
            share = (grown / jnp.sum(grown, axis=1, keepdims=True)).astype(BF16)
            spread[pl.ds(b * PATCHES, PATCHES), :] = lax.dot_general(
                share, order[:, pl.ds(b * E, E)], (((1,), (1,)), ((), ())), preferred_element_type=F32
            ).astype(BF16)
        pltpu.make_async_copy(spread, spread_h, out_sem).start()

        copies[5].wait()
        words[:, pl.ds(0, 128)] = jnp.right_shift(kb[...], 5).astype(F32).astype(BF16)
        words[:, pl.ds(128, 128)] = jnp.bitwise_and(kb[...], 31).astype(F32).astype(BF16)
        for i in (6, 7, 8):
            copies[i].wait()
        keep_flags(0)

    def turn(t, carry):
        for lag, stage in stages:
            g = t - lag
            pl.when(jnp.logical_and(g >= 0, g < GROUPS))(functools.partial(stage, g))
        pl.when(t == 0)(prepare)
        return carry

    lax.fori_loop(0, GROUPS + max(lag for lag, _ in stages), turn, 0)

    pltpu.make_async_copy(spread, spread_h, out_sem).wait()
    remote = slots.at[pl.ds(0, PLANE - 1)]
    arrived(remote, xa_send)
    arrived(za, z_send)
    arrived(part.at[pl.ds(0, 3)], f_send)
    arrived(other, q_send)
    arrived(part.at[pl.ds(0, 3)], t_send)
    arrived(remote, xb_send)
    for g in range(GROUPS):
        arrived(out_h.at[pl.ds(0, UNITS)], xb_recv.at[g])


def exchange(images, router, w_in, w_out, words):
    order = jnp.asarray(slot_order(), BF16)
    pairs = jnp.asarray(pair_order(), BF16)
    bits = jnp.asarray(bit_table(), BF16)
    anywhere = pl.BlockSpec(memory_space=pl.ANY)
    dma = pltpu.SemaphoreType.DMA
    return pl.pallas_call(
        kernel,
        out_shape=(
            jax.ShapeDtypeStruct((PLANE, 16, D), BF16),
            jax.ShapeDtypeStruct((IMG * PATCHES, IMG * E), BF16),
        ),
        in_specs=[anywhere] * 8,
        out_specs=(anywhere, anywhere),
        scratch_shapes=[
            pltpu.VMEM((IMG, PATCHES, D), BF16),
            pltpu.VMEM((D, E), BF16),
            pltpu.VMEM((D, D), BF16),
            pltpu.VMEM((D, D), BF16),
            pltpu.VMEM((IMAGES, 128), jnp.int32),
            pltpu.VMEM((512, 512), BF16),
            pltpu.VMEM((64, 64), BF16),
            pltpu.VMEM((256, D), BF16),
            pltpu.VMEM((IMAGES, 256), BF16),
            pltpu.VMEM((IMG, PATCHES, E), F32),
            pltpu.VMEM((IMG * E, D), BF16),
            pltpu.VMEM((PLANE, 16, D), BF16),
            pltpu.VMEM((UNITS, 16, D), BF16),
            pltpu.VMEM((GROUPS, UNITS, 16, D), BF16),
            pltpu.VMEM((GROUPS, PAIRS, 16, D), BF16),
            pltpu.VMEM((GROUPS, 8, 16, D), BF16),
            pltpu.VMEM((GROUPS, 8, 16, D), BF16),
            pltpu.VMEM((GROUPS, 4, 16, D), BF16),
            pltpu.VMEM((GROUPS, 4, 16, D), BF16),
            pltpu.VMEM((GROUPS, PAIRS, 16, D), BF16),
            pltpu.VMEM((GROUPS, UNITS, 16, D), BF16),
            pltpu.VMEM((128, D), BF16),
            pltpu.VMEM((128, D), BF16),
            pltpu.VMEM((IMG * PATCHES, IMG * E), BF16),
            dma((9,)),
            dma, dma((GROUPS,)),
            dma, dma((GROUPS, 3)),
            dma, dma((GROUPS,)),
            dma, dma((GROUPS,)),
            dma, dma((GROUPS,)),
            dma, dma((GROUPS,)),
            dma,
        ],
        compiler_params=pltpu.CompilerParams(
            collective_id=0, has_side_effects=True, vmem_limit_bytes=60 * 2**20
        ),
    )(images, router, w_in, w_out, words, order, pairs, bits)


def on_device(images, router, w_in, w_out, keep_bits):
    words = keep_bits.reshape(IMAGES, 128)
    arrived, spread = exchange(images, router, w_in, w_out, words)
    mixed = jnp.dot(spread, arrived.reshape(512, D), preferred_element_type=F32)
    return mixed.astype(BF16).reshape(IMG, PATCHES, D)


def solution(mesh):
    placed = (
        P(("dp", "expert"), None, None),
        P(),
        P(("dp", "expert"), None, None),
        P(("dp", "expert"), None, None),
        P(None, ("dp", "expert"), None),
    )
    return jax.shard_map(
        on_device,
        mesh=mesh,
        in_specs=placed,
        out_specs=P(("dp", "expert"), None, None),
        check_vma=False,
    )
```

```python
import functools

import jax
import jax.numpy as jnp
import numpy as np
from jax import lax
from jax.experimental import pallas as pl
from jax.experimental.pallas import tpu as pltpu
from jax.sharding import PartitionSpec as P

GROUPS = 8
PLANE = 32
UNITS = 4
AHEAD = 2
OFFSETS = (
    (0, 0), (1, 0), (0, 1), (0, 3), (2, 0), (0, 2), (2, 1), (2, 3),
    (1, 2), (3, 2), (2, 2), (3, 3), (1, 3), (3, 1), (3, 0), (1, 1),
)
PAIRS = 4
IMG = 4
PATCHES = 256
D = 1280
E = 128
IMAGES = 1024
TILE = 256
MESH = pl.DeviceIdType.MESH
KEEP_RATE = 0.875
BF16 = jnp.bfloat16
F32 = jnp.float32


def slot_order():
    table = np.zeros((PLANE * PAIRS * IMG, IMG * E), np.float32)
    for s in range(PLANE):
        for q in range(PAIRS):
            local = (s // 8) * 16 + (s % 2) * 8 + (s // 2 % 4) * 2
            expert = (q // 2) * 64 + local + q % 2
            for b in range(IMG):
                table[(s * PAIRS + q) * IMG + b, b * E + expert] = 1.0
    return table


def pair_order():
    table = np.zeros((64, 64), np.float32)
    for q in range(PAIRS):
        for u in range(UNITS):
            for b in range(IMG):
                table[(q * UNITS + u) * IMG + b, (u * PAIRS + q) * IMG + b] = 1.0
    return table


def bit_table():
    table = np.zeros((256, D), np.float32)
    for w in range(128):
        for i in range(10):
            table[w, 10 * w + i] = 32.0 / 2**i
            table[128 + w, 10 * w + i] = 1.0 / 2**i
    return table


def offset(g, chip):
    if isinstance(g, int):
        return OFFSETS[2 * g + chip]
    dx, dy = OFFSETS[chip]
    for i in range(1, GROUPS):
        here = g == i
        dx = jnp.where(here, OFFSETS[2 * i + chip][0], dx)
        dy = jnp.where(here, OFFSETS[2 * i + chip][1], dy)
    return dx, dy


def kernel(
    img_h, router_h, w1_h, w2_h, kb_h, order_h, pairs_h, bits_h,
    out_h, spread_h,
    img, router, w1, w2, kb, order, pairs, bits, words, logits, raw, slots, first_slots,
    xa, za, rows, part, other, total, back, xb, hidden, keep, spread,
    load_sem, xa_send, xa_recv, z_send, z_recv, f_send, f_recv,
    q_send, q_recv, t_send, t_recv, xb_send, xb_recv, out_sem,
):
    dp = lax.axis_index("dp")
    ex = lax.axis_index("expert")
    core = lax.rem(dp, 2)
    y = lax.rem(lax.div(dp, 2), 4)
    z = lax.div(dp, 8) * 4 + lax.rem(ex, 4)
    x = lax.div(ex, 4)
    me = (y * 4 + x) * 2 + core
    pair = lax.div(z, 2)
    sg = 2 * lax.rem(z, 2) - 1

    def at(s, zz):
        return (
            lax.div(zz, 4) * 8 + lax.div(s, 8) * 2 + lax.rem(s, 2),
            lax.rem(lax.div(s, 2), 4) * 4 + lax.rem(zz, 4),
        )

    def along_z(step):
        return lax.rem(z + step * sg + 8, 8)

    def chip_at(g, chip, sign):
        dx, dy = offset(g, chip)
        return lax.rem(y + sign * dy + 4, 4) * 4 + lax.rem(x + sign * dx + 4, 4)

    def device_at(g, unit, sign):
        side = core if unit % 2 == 0 else 1 - core
        return chip_at(g, unit // 2, sign) * 2 + side

    loads = [
        (img_h.at[pl.ds(0, 2)], img.at[pl.ds(0, 2)]),
        (router_h, router),
        (img_h.at[pl.ds(2, 2)], img.at[pl.ds(2, 2)]),
        (order_h, order),
        (pairs_h, pairs),
        (kb_h, kb),
        (bits_h, bits),
        (w1_h.at[0], w1),
        (w2_h.at[0], w2),
    ]
    copies = [
        pltpu.make_async_copy(src, dst, load_sem.at[i]) for i, (src, dst) in enumerate(loads)
    ]
    for copy in copies[:3]:
        copy.start()

    barrier = pltpu.get_barrier_semaphore()
    partners = []
    for g in range(GROUPS):
        for u in range(UNITS):
            if g or u:
                partners.append(at(device_at(g, u, 1), z))
    for step in (1, 2, 3, -1, -2):
        partners.append(at(me, along_z(step)))
    for partner in partners:
        pl.semaphore_signal(barrier, inc=1, device_id=partner, device_id_type=MESH)

    copies[1].wait()
    for half in range(2):
        copies[2 * half].wait()
        if half == 0:
            copies[3].start()
        both = jnp.dot(
            img[pl.ds(2 * half, 2)].reshape(2 * PATCHES, D), router[...],
            preferred_element_type=F32,
        )
        for b in (2 * half, 2 * half + 1):
            scores = both[(b % 2) * PATCHES : (b % 2 + 1) * PATCHES]
            logits[b] = scores
            top = jnp.max(scores, axis=0, keepdims=True)
            grown = jnp.exp(scores - top)
            share = (grown / jnp.sum(grown, axis=0, keepdims=True)).astype(BF16)
            for n in range(D // TILE):
                cols = pl.ds(n * TILE, TILE)
                raw[pl.ds(b * E, E), cols] = lax.dot_general(
                    share, img[b, :, cols], (((0,), (0,)), ((), ())), preferred_element_type=F32
                ).astype(BF16)

    for copy in copies[4:]:
        copy.start()
    copies[3].wait()
    near = jnp.concatenate(
        [order[pl.ds(pl.multiple_of(chip_at(0, c, 1) * 32, 32), 32), :] for c in range(2)], axis=0
    )
    for n in range(D // TILE):
        cols = pl.ds(n * TILE, TILE)
        first_slots[:, :, cols] = (
            jnp.dot(near, raw[:, cols], preferred_element_type=F32)
            .astype(BF16)
            .reshape(UNITS, 16, TILE)
        )
    pl.semaphore_wait(barrier, len(partners))

    def send_plane(g):
        for u in range(UNITS):
            s = device_at(g, u, 1)
            land = xa.at[g, (u // 2) * 2 + core]
            early = isinstance(g, int) and g == 0
            if early:
                src = first_slots.at[(u // 2) * 2 + lax.rem(s, 2)]
            else:
                src = slots.at[s]
            if early and u == 0:
                pltpu.make_async_copy(src, land, xa_recv.at[g]).start()
            else:
                pltpu.make_async_remote_copy(
                    src, land, xa_send, xa_recv.at[g],
                    device_id=at(s, z), device_id_type=MESH,
                ).start()

    send_plane(0)
    for n in range(D // TILE):
        cols = pl.ds(n * TILE, TILE)
        slots[:, :, cols] = (
            jnp.dot(order[...], raw[:, cols], preferred_element_type=F32)
            .astype(BF16)
            .reshape(PLANE, 16, TILE)
        )
    for g in range(1, AHEAD):
        send_plane(g)

    copies[4].wait()

    def arrived(ref, sem):
        pltpu.make_async_copy(ref, ref, sem).wait()

    def send(src, dst, send_sem, recv_sem, zz):
        pltpu.make_async_remote_copy(
            src, dst, send_sem, recv_sem, device_id=at(me, zz), device_id_type=MESH
        ).start()

    def dispatch(g):
        arrived(xa.at[g], xa_recv.at[g])
        for n in range(D // TILE):
            cols = pl.ds(n * TILE, TILE)
            za[g, :, :, cols] = (
                jnp.dot(
                    pairs[...], xa[g, :, :, cols].reshape(64, TILE), preferred_element_type=F32
                )
                .astype(BF16)
                .reshape(PAIRS, 16, TILE)
            )
        send(za.at[g, pair], rows.at[g, 4], z_send, f_recv.at[g], along_z(-1))
        for slot, step in ((3, 3), (2, -2), (1, 1)):
            zz = along_z(step)
            send(
                za.at[g, lax.div(zz, 2)], rows.at[g, slot],
                z_send, z_recv.at[g, slot - 1], zz,
            )
        pl.when(g + AHEAD < GROUPS)(functools.partial(send_plane, g + AHEAD))
        rows[g, 0] = za[g, pair]

    def keep_flags(g):
        r = lax.broadcasted_iota(jnp.int32, (128, 1), 0)
        j = jnp.right_shift(r, 4)
        side = jnp.bitwise_and(jnp.right_shift(r, 2), 1)
        zz = jnp.bitwise_and(jnp.where(j < 4, z + j * sg, z - (j - 3) * sg) + 8, 7)
        near, far = chip_at(g, 0, -1), chip_at(g, 1, -1)
        chip = jnp.where(jnp.bitwise_and(r, 8) == 0, near, far)
        group = jnp.right_shift(zz, 2) * 8 + jnp.right_shift(chip, 2) * 2 + side
        device = group * 16 + jnp.bitwise_and(chip, 3) * 4 + jnp.bitwise_and(zz, 3)
        image = device * IMG + jnp.bitwise_and(r, 3)
        c = lax.broadcasted_iota(jnp.int32, (128, IMAGES), 1)
        pick = jnp.where(c == image, 1.0, 0.0).astype(BF16)
        mine = jnp.dot(pick, words[...], preferred_element_type=F32).astype(BF16)

        def tile(n, carry):
            cols = pl.ds(pl.multiple_of(n * TILE, TILE), TILE)
            value = jnp.dot(mine, bits[:, cols], preferred_element_type=F32)
            flag = jnp.bitwise_and(value.astype(jnp.int32), 1)
            keep[:, cols] = flag.astype(F32).astype(BF16)
            return carry

        lax.fori_loop(0, D // TILE, tile, 0, unroll=True)

    def forward(g):
        for j in (3, 2, 1):
            arrived(rows.at[g, j], z_recv.at[g, j - 1])
            send(rows.at[g, j], rows.at[g, 4 + j], f_send, f_recv.at[g], along_z(-1))

    def experts(g):
        arrived(rows.at[g, pl.ds(4, 4)], f_recv.at[g])

        def first(n, carry):
            cols = pl.ds(pl.multiple_of(n * TILE, TILE), TILE)
            value = jnp.dot(rows[g].reshape(128, D), w1[:, cols], preferred_element_type=F32)
            flag = keep[:, cols].astype(F32)
            hidden[:, cols] = (jax.nn.gelu(value) * flag * (1.0 / KEEP_RATE)).astype(BF16)
            return carry

        def second(n, carry):
            cols = pl.ds(pl.multiple_of(n * TILE, TILE), TILE)
            value = jnp.dot(hidden[...], w2[:, cols], preferred_element_type=F32)
            part[g, :, :, cols] = value.astype(BF16).reshape(8, 16, TILE)
            return carry

        lax.fori_loop(0, D // TILE, first, 0, unroll=True)
        lax.fori_loop(0, D // TILE, second, 0, unroll=True)
        send(part.at[g, pl.ds(4, 4)], other.at[g], q_send, q_recv.at[g], along_z(-1))
        pl.when(g + 1 < GROUPS)(functools.partial(keep_flags, g + 1))

    def gather_pair(g):
        arrived(other.at[g], q_recv.at[g])
        for j in (3, 2, 1):
            total[g, j] = (part[g, j].astype(F32) + other[g, j].astype(F32)).astype(BF16)
            send(total.at[g, j], back.at[g, pair], t_send, t_recv.at[g], along_z(j))
        back[g, pair] = (part[g, 0].astype(F32) + other[g, 0].astype(F32)).astype(BF16)

    def give_back(g):
        arrived(back.at[g, pl.ds(0, 3)], t_recv.at[g])
        for n in range(D // TILE):
            cols = pl.ds(n * TILE, TILE)
            xb[g, :, :, cols] = (
                lax.dot_general(
                    pairs[...], back[g, :, :, cols].reshape(64, TILE),
                    (((0,), (0,)), ((), ())), preferred_element_type=F32,
                )
                .astype(BF16)
                .reshape(UNITS, 16, TILE)
            )
        for u in range(UNITS):
            s = device_at(g, u, -1)
            gone = xb.at[g, (u // 2) * 2 + (core if u % 2 == 0 else 1 - core)]
            land = xb_recv.at[g]

            def start_remote(s=s, gone=gone, land=land):
                pltpu.make_async_remote_copy(
                    gone, out_h.at[me], xb_send, land,
                    device_id=at(s, z), device_id_type=MESH,
                ).start()

            if u:
                start_remote()
            else:

                @pl.when(g == 0)
                def _(gone=gone, land=land):
                    pltpu.make_async_copy(gone, out_h.at[me], land).start()

                pl.when(g > 0)(start_remote)

    stages = (
        (0, dispatch),
        (1, forward),
        (3, experts),
        (4, gather_pair),
        (5, give_back),
    )

    def prepare():
        for b in range(IMG):
            scores = logits[b]
            grown = jnp.exp(scores - jnp.max(scores, axis=1, keepdims=True))
            share = (grown / jnp.sum(grown, axis=1, keepdims=True)).astype(BF16)
            spread[pl.ds(b * PATCHES, PATCHES), :] = lax.dot_general(
                share, order[:, pl.ds(b * E, E)], (((1,), (1,)), ((), ())), preferred_element_type=F32
            ).astype(BF16)
        pltpu.make_async_copy(spread, spread_h, out_sem).start()

        copies[5].wait()
        words[:, pl.ds(0, 128)] = jnp.right_shift(kb[...], 5).astype(F32).astype(BF16)
        words[:, pl.ds(128, 128)] = jnp.bitwise_and(kb[...], 31).astype(F32).astype(BF16)
        for i in (6, 7, 8):
            copies[i].wait()
        keep_flags(0)

    def turn(t, carry):
        for lag, stage in stages:
            g = t - lag
            pl.when(jnp.logical_and(g >= 0, g < GROUPS))(functools.partial(stage, g))
        pl.when(t == 0)(prepare)
        return carry

    lax.fori_loop(0, GROUPS + max(lag for lag, _ in stages), turn, 0)

    pltpu.make_async_copy(spread, spread_h, out_sem).wait()
    remote = slots.at[pl.ds(0, PLANE - 1)]
    arrived(remote, xa_send)
    arrived(za, z_send)
    arrived(part.at[pl.ds(0, 3)], f_send)
    arrived(other, q_send)
    arrived(part.at[pl.ds(0, 3)], t_send)
    arrived(remote, xb_send)
    for g in range(GROUPS):
        arrived(out_h.at[pl.ds(0, UNITS)], xb_recv.at[g])


def exchange(images, router, w_in, w_out, words):
    order = jnp.asarray(slot_order(), BF16)
    pairs = jnp.asarray(pair_order(), BF16)
    bits = jnp.asarray(bit_table(), BF16)
    anywhere = pl.BlockSpec(memory_space=pl.ANY)
    dma = pltpu.SemaphoreType.DMA
    return pl.pallas_call(
        kernel,
        out_shape=(
            jax.ShapeDtypeStruct((PLANE, 16, D), BF16),
            jax.ShapeDtypeStruct((IMG * PATCHES, IMG * E), BF16),
        ),
        in_specs=[anywhere] * 8,
        out_specs=(anywhere, anywhere),
        scratch_shapes=[
            pltpu.VMEM((IMG, PATCHES, D), BF16),
            pltpu.VMEM((D, E), BF16),
            pltpu.VMEM((D, D), BF16),
            pltpu.VMEM((D, D), BF16),
            pltpu.VMEM((IMAGES, 128), jnp.int32),
            pltpu.VMEM((512, 512), BF16),
            pltpu.VMEM((64, 64), BF16),
            pltpu.VMEM((256, D), BF16),
            pltpu.VMEM((IMAGES, 256), BF16),
            pltpu.VMEM((IMG, PATCHES, E), F32),
            pltpu.VMEM((IMG * E, D), BF16),
            pltpu.VMEM((PLANE, 16, D), BF16),
            pltpu.VMEM((UNITS, 16, D), BF16),
            pltpu.VMEM((GROUPS, UNITS, 16, D), BF16),
            pltpu.VMEM((GROUPS, PAIRS, 16, D), BF16),
            pltpu.VMEM((GROUPS, 8, 16, D), BF16),
            pltpu.VMEM((GROUPS, 8, 16, D), BF16),
            pltpu.VMEM((GROUPS, 4, 16, D), BF16),
            pltpu.VMEM((GROUPS, 4, 16, D), BF16),
            pltpu.VMEM((GROUPS, PAIRS, 16, D), BF16),
            pltpu.VMEM((GROUPS, UNITS, 16, D), BF16),
            pltpu.VMEM((128, D), BF16),
            pltpu.VMEM((128, D), BF16),
            pltpu.VMEM((IMG * PATCHES, IMG * E), BF16),
            dma((9,)),
            dma, dma((GROUPS,)),
            dma, dma((GROUPS, 3)),
            dma, dma((GROUPS,)),
            dma, dma((GROUPS,)),
            dma, dma((GROUPS,)),
            dma, dma((GROUPS,)),
            dma,
        ],
        compiler_params=pltpu.CompilerParams(
            collective_id=0, has_side_effects=True, vmem_limit_bytes=60 * 2**20
        ),
    )(images, router, w_in, w_out, words, order, pairs, bits)


def on_device(images, router, w_in, w_out, keep_bits):
    words = keep_bits.reshape(IMAGES, 128)
    arrived, spread = exchange(images, router, w_in, w_out, words)
    mixed = jnp.dot(spread, arrived.reshape(512, D), preferred_element_type=F32)
    return mixed.astype(BF16).reshape(IMG, PATCHES, D)


def solution(mesh):
    placed = (
        P(("dp", "expert"), None, None),
        P(),
        P(("dp", "expert"), None, None),
        P(("dp", "expert"), None, None),
        P(None, ("dp", "expert"), None),
    )
    return jax.shard_map(
        on_device,
        mesh=mesh,
        in_specs=placed,
        out_specs=P(("dp", "expert"), None, None),
        check_vma=False,
    )
```
